256 devices in a mesh: prompt: 16 (over z, core), comp: 16 (over x, y).
Axes of the slice: x: 4, y: 4, z: 8, core: 2. Of those that a mesh axis runs over, the one named last changes fastest.
Arguments:
- prompt_inner: bfloat16 [4096, 16384], P('prompt', 'comp'), may hold values from -0.59765625 to 0.59765625
- prompt_proj: bfloat16 [4096, 4096], P('prompt'), may hold values from -0.8984375 to 0.8984375
- prompt_step: float32 [256, 4096], P('comp', 'prompt')
- completion_inner: bfloat16 [32, 256, 16384], P('comp', None, 'prompt'), may hold values from -0.59765625 to 0.59765625
- completion_gate: bfloat16 [32, 256, 16384], P('comp', None, 'prompt'), may hold values from -12 to 12
- completion_projections: bfloat16 [32, 256, 4096], P('comp'), may hold values from -0.8984375 to 0.8984375
- sample_step: float32 [256, 32, 256], P('prompt', 'comp')
- sample_length: int32 [32], P('comp'), may hold values from 1 to 256, as said below
- decay_log: float32 [256], replicated
- conv_inner: bfloat16 [4, 16384], replicated, may hold values from -3 to 3
- conv_proj: bfloat16 [4, 4096], replicated, may hold values from -3 to 3
- norm_gain: float32 [16384], P('prompt'), may hold values from 0.5 to 1.5
Outputs:
- sample_out: bfloat16 [32, 256, 16384], P('comp', None, 'prompt')
The draws below stay inside these ranges and needn't reach their ends.
Inputs may be any that keep to these rules, and one draw needn't show every extreme that they name: `sample_length`: some completion slot is full.
All inputs are finite; a program needn't handle non-finite values.
Results may differ from the reference program's by a relative error of at most 0.014.
Values may be sent and summed in bfloat16 or wider, within the bound.
A program may use at most 128 MiB of HBM per device.

```python
import jax
import jax.numpy as jnp
from jax import lax

STATE_HEADS = 256
HEAD_WIDTH = 64
STATE_WIDTH = 256
STATE_GROUPS = 8
CONV = 4
BLOCK = 128
SAMPLE_POSITIONS = 256
PTOK = 4096
SLOT_TOTAL = 32


def head_rates(key):
    base_key = jax.random.fold_in(key, 11)
    slow_share = 0.5
    slow_pick = jax.random.uniform(jax.random.fold_in(base_key, 1), (STATE_HEADS,), jnp.float32) < slow_share
    slow_rate = jnp.exp(jax.random.uniform(jax.random.fold_in(base_key, 3), (STATE_HEADS,), jnp.float32, jnp.log(0.3), jnp.log(1.2))) / (PTOK + SAMPLE_POSITIONS)
    fast_rate = jnp.exp(jax.random.uniform(jax.random.fold_in(base_key, 4), (STATE_HEADS,), jnp.float32, jnp.log(0.002), jnp.log(0.035)))
    rate_vals = jnp.where(slow_pick, slow_rate, fast_rate)
    step_factor = jnp.exp(jax.random.uniform(jax.random.fold_in(base_key, 2), (STATE_HEADS,), jnp.float32, jnp.log(0.7), jnp.log(1.4)))
    step_mean = 3.0 * jnp.sqrt(rate_vals) * step_factor
    return (jnp.log(rate_vals / step_mean), step_mean)


def unscaled_steps(key, salt, shape):
    _, step_mean = head_rates(key)
    noise_vals = jax.random.truncated_normal(jax.random.fold_in(key, salt), -3.0, 3.0, shape, jnp.float32)
    step_vals = step_mean.reshape((STATE_HEADS,) + (1,) * (len(shape) - 1)) * jnp.exp(0.5 * noise_vals)
    return jnp.log(jnp.expm1(step_vals))


def draw_decay_log(key, part):
    return head_rates(key)[0]


def draw_prompt_step(key, part):
    return unscaled_steps(key, 21, (STATE_HEADS, PTOK))


def draw_sample_step(key, part):
    return unscaled_steps(key, 22, (STATE_HEADS, SLOT_TOTAL, SAMPLE_POSITIONS))


def draw_sample_length(key, part):
    sample_lengths = jax.random.randint(jax.random.fold_in(key, 31), (SLOT_TOTAL,), 1, SAMPLE_POSITIONS + 1)
    whole_slot = jax.random.randint(jax.random.fold_in(key, 32), (), 0, SLOT_TOTAL)
    return jnp.where(jnp.arange(SLOT_TOTAL) == whole_slot, SAMPLE_POSITIONS, sample_lengths).astype(jnp.int32)


def level_of(rng, dims, pieces, low, high):
    level, own = 1.0, jax.random.fold_in(rng, 6)
    for position, shards_of in pieces:
        draws = jnp.exp(jax.random.uniform(jax.random.fold_in(own, position), (shards_of,), jnp.float32, low / len(pieces), high / len(pieces)))
        level = level * jnp.repeat(draws, dims[position] // shards_of).reshape([-1 if axis == position else 1 for axis in range(len(dims))])
    return level


def gaussian(rng, dims, deviation, limit, split=(), held_as=jnp.bfloat16):
    entries = deviation * jax.random.normal(rng, dims, jnp.float32)
    if split:
        entries = entries * level_of(rng, dims, split, -0.22, 0.18)
    return jnp.clip(entries, -limit, limit).astype(held_as)


def setup_inputs(seed: int = 0) -> dict:
    keys = jax.random.split(jax.random.key(seed), 13)
    return {
        "prompt_inner": gaussian(keys[0], (PTOK, STATE_HEADS * HEAD_WIDTH), 0.1, 0.59765625, ((0, 16), (1, 16))),
        "prompt_proj": gaussian(keys[1], (PTOK, 2 * STATE_GROUPS * STATE_WIDTH), 0.15, 0.8984375, ((0, 16),)),
        "prompt_step": draw_prompt_step(jax.random.fold_in(keys[12], 71), 0),
        "completion_inner": gaussian(keys[3], (SLOT_TOTAL, SAMPLE_POSITIONS, STATE_HEADS * HEAD_WIDTH), 0.1, 0.59765625, ((0, 16), (2, 16))),
        "completion_gate": gaussian(keys[4], (SLOT_TOTAL, SAMPLE_POSITIONS, STATE_HEADS * HEAD_WIDTH), 2.0, 12.0, ((0, 16), (2, 16))),
        "completion_projections": gaussian(keys[5], (SLOT_TOTAL, SAMPLE_POSITIONS, 2 * STATE_GROUPS * STATE_WIDTH), 0.15, 0.8984375, ((0, 16),)),
        "sample_step": draw_sample_step(jax.random.fold_in(keys[12], 71), 0),
        "sample_length": draw_sample_length(jax.random.fold_in(keys[12], 71), 0),
        "decay_log": draw_decay_log(jax.random.fold_in(keys[12], 71), 0),
        "conv_inner": gaussian(keys[9], (CONV, STATE_HEADS * HEAD_WIDTH), CONV ** -0.5, 3.0),
        "conv_proj": gaussian(keys[10], (CONV, 2 * STATE_GROUPS * STATE_WIDTH), CONV ** -0.5, 3.0),
        "norm_gain": jnp.clip(1.0 + 0.1 * jax.random.normal(keys[11], (STATE_HEADS * HEAD_WIDTH,), jnp.float32), 0.5, 1.5),
    }


EPS = 1e-05
HIGHEST = lax.Precision.HIGHEST

def causal_conv(source, kernel, leading):
    padded = jnp.concatenate([leading, source], axis=0).astype(jnp.float32)
    kernel_wide = kernel.astype(jnp.float32)
    row_count = source.shape[0]
    summed = jnp.zeros(source.shape, jnp.float32)
    for offset in range(kernel.shape[0]):
        summed = summed + kernel_wide[offset] * padded[offset:offset + row_count]
    return jax.nn.silu(summed).astype(jnp.bfloat16)

def block_exact(state_in, inner_blk, b_blk, c_blk, step_blk, rate_vals):
    cumul = jnp.cumsum(-rate_vals[:, :, None] * step_blk, axis=2)
    scores = jnp.einsum('ign,jgn->gij', c_blk.astype(jnp.float32), b_blk.astype(jnp.float32), precision=HIGHEST)
    spread_log = cumul[:, :, :, None] - cumul[:, :, None, :]
    length_q = step_blk.shape[2]
    causal = jnp.arange(length_q)[:, None] >= jnp.arange(length_q)[None, :]
    decay_mat = jnp.exp(jnp.where(causal, spread_log, -jnp.inf))
    mixer_w = (scores[:, None] * decay_mat * step_blk[:, :, None, :]).astype(jnp.bfloat16)
    intra_part = jnp.einsum('gkij,jgkd->igkd', mixer_w.astype(jnp.float32), inner_blk.astype(jnp.float32), precision=HIGHEST)
    readout = jnp.einsum('ign,gkdn->igkd', c_blk.astype(jnp.float32), state_in, precision=HIGHEST)
    inter_part = jnp.transpose(jnp.exp(cumul), (2, 0, 1))[..., None] * readout
    weights = jnp.exp(cumul[:, :, -1:] - cumul) * step_blk
    packed = (inner_blk.astype(jnp.float32) * jnp.transpose(weights, (2, 0, 1))[..., None]).astype(jnp.bfloat16)
    fresh_part = jnp.einsum('jgn,jgkd->gkdn', b_blk.astype(jnp.float32), packed.astype(jnp.float32), precision=HIGHEST)
    return (intra_part + inter_part, jnp.exp(cumul[:, :, -1])[..., None, None] * state_in + fresh_part)

def reference(prompt_inner, prompt_proj, prompt_step, completion_inner, completion_gate, completion_projections, sample_step, sample_length, decay_log, conv_inner, conv_proj, norm_gain):
    heads_group = STATE_HEADS // STATE_GROUPS
    state_feats = STATE_GROUPS * STATE_WIDTH
    lag_rows = CONV - 1
    rate_all = jnp.exp(decay_log)
    lead_inner = jnp.zeros((lag_rows, STATE_HEADS * HEAD_WIDTH), jnp.bfloat16)
    lead_proj = jnp.zeros((lag_rows, state_feats), jnp.bfloat16)
    prompt_conv = causal_conv(prompt_inner, conv_inner, lead_inner)
    prompt_b = causal_conv(prompt_proj[:, :state_feats], conv_proj[:, :state_feats], lead_proj)
    prompt_dt = jax.nn.softplus(prompt_step)
    prompt_cum = jnp.cumsum(-rate_all[:, None] * prompt_dt, axis=1)
    weight_p = jnp.exp(prompt_cum[:, -1:] - prompt_cum) * prompt_dt
    scaled = prompt_conv.astype(jnp.float32).reshape(PTOK, STATE_HEADS, HEAD_WIDTH) * jnp.transpose(weight_p)[:, :, None]
    scaled = scaled.reshape(PTOK, STATE_GROUPS, heads_group, HEAD_WIDTH)
    b_groups = prompt_b.astype(jnp.float32).reshape(PTOK, STATE_GROUPS, STATE_WIDTH)
    prompt_state = jnp.einsum('tgn,tghd->ghdn', b_groups, scaled, precision=HIGHEST)
    tail_inner = prompt_inner[PTOK - lag_rows:]
    tail_proj = prompt_proj[PTOK - lag_rows:]
    block_count = SAMPLE_POSITIONS // BLOCK
    rate_grid = rate_all.reshape(STATE_GROUPS, heads_group)

    def one_sample(slot_args):
        inner_in, gate_in, proj_in, step_raw, live_len = slot_args
        inner_conv = causal_conv(inner_in, conv_inner, tail_inner)
        proj_conv = causal_conv(proj_in, conv_proj, tail_proj)
        b_blocks = proj_conv[:, :state_feats].reshape(block_count, BLOCK, STATE_GROUPS, STATE_WIDTH)
        c_blocks = proj_conv[:, state_feats:].reshape(block_count, BLOCK, STATE_GROUPS, STATE_WIDTH)
        inner_blocks = inner_conv.reshape(block_count, BLOCK, STATE_GROUPS, heads_group, HEAD_WIDTH)
        step_blocks = jnp.transpose(jax.nn.softplus(step_raw).reshape(STATE_GROUPS, heads_group, block_count, BLOCK), (2, 0, 1, 3))

        def advance(carry, block_in):
            block_out, carry_next = block_exact(carry, block_in[0], block_in[1], block_in[2], block_in[3], rate_grid)
            return (carry_next, block_out)
        _, block_outs = lax.scan(advance, prompt_state, (inner_blocks, b_blocks, c_blocks, step_blocks))
        ssm_out = block_outs.reshape(SAMPLE_POSITIONS, STATE_HEADS * HEAD_WIDTH)
        gated = ssm_out * jax.nn.silu(gate_in.astype(jnp.float32))
        grouped = gated.reshape(SAMPLE_POSITIONS, STATE_GROUPS, heads_group * HEAD_WIDTH)
        mean_square = lax.optimization_barrier(jnp.mean(grouped * grouped, axis=2, keepdims=True))
        result = (grouped * lax.rsqrt(mean_square + EPS)).reshape(SAMPLE_POSITIONS, STATE_HEADS * HEAD_WIDTH) * norm_gain[None, :]
        live_rows = jnp.arange(SAMPLE_POSITIONS) < live_len
        return jnp.where(live_rows[:, None], result, 0.0).astype(jnp.bfloat16)
    return lax.map(one_sample, (completion_inner, completion_gate, completion_projections, jnp.transpose(sample_step, (1, 0, 2)), sample_length))
```

```python
import functools

import jax
import jax.numpy as jnp
from jax import lax
from jax.experimental import pallas as pl
from jax.experimental.pallas import tpu as pltpu
from jax.sharding import PartitionSpec as P

STATE_HEADS = 256
HEAD_WIDTH = 64
STATE_WIDTH = 256
STATE_GROUPS = 8
CONV = 4
EPS = 1e-05
LOG2E = 1.4426950408889634

MESH = pl.DeviceIdType.MESH
F32 = jnp.float32
BF16 = jnp.bfloat16

ROWS = 16
COLS = 16
CHIPS = 8
TOK = 256
FEAT = 1024
HALF = 512
GROUP_HEADS = 32
PROJ_C = STATE_GROUPS * STATE_WIDTH

R_SIB, R_HALO, R_TAIL, R_RED, R_LOG, R_AG, R_SQ = 0, 3, 5, 8, 16, 24, 40
N_RECV = 42
S_SIB, S_HALO, S_TX, S_TB, S_TC, S_RED, S_LOG, S_AG, S_SQ = 0, 3, 7, 23, 38, 53, 61, 69, 84
N_SEND = 86
(L_PX, L_PB, L_PS, L_WX, L_WB, L_CX, L_CG, L_CB, L_CC, L_SS, L_WCX, L_WCB, L_WCC, L_TX, L_TB, L_TC, L_OUT) = range(17)
N_LOCAL = 18


def silu(v):
    h = 0.5 * v
    return h + h * jnp.tanh(h)


def softplus(v):
    return jnp.maximum(v, 0.0) + jnp.log1p(jnp.exp(-jnp.abs(v)))


def split3(v):
    a = v.astype(BF16)
    r = v - a.astype(F32)
    b = r.astype(BF16)
    c = (r - b.astype(F32)).astype(BF16)
    return a, b, c


def dot_nt(a, b):
    return lax.dot_general(a, b, (((1,), (1,)), ((), ())), preferred_element_type=F32)


def dot_tn(a, b):
    return lax.dot_general(a, b, (((0,), (0,)), ((), ())), preferred_element_type=F32)


def causal_conv(src, lead, taps):
    x = jnp.concatenate([lead.astype(F32)[8:], src.astype(F32)], axis=0)
    total = x * taps[3:4]
    for lag in (1, 2, 3):
        total = total + pltpu.roll(x, lag, 0) * taps[3 - lag : 4 - lag]
    return silu(total[8:])


def pick_rows(row, first, count):
    lanes = lax.broadcasted_iota(jnp.int32, (count, row.shape[1]), 1)
    heads = first + lax.broadcasted_iota(jnp.int32, (count, row.shape[1]), 0)
    wide = jnp.broadcast_to(row, (count, row.shape[1]))
    return jnp.sum(jnp.where(lanes == heads, wide, 0.0), axis=1, keepdims=True)


def kernel(
    inner, proj, pstep, cin, gate, cproj, sstep, slen, dlog, cvi, cvp, gain, out,
    px, pb, ps, hx, hb, wx, wb, cx, cg, cbc, ss, wcx, wcbc, tx, tbc,
    st, logs, red, redlog, stf, xcv, bcv, part, coef, scores, sq, sqs, obuf,
    lsem, ssem, rsem,
):
    p = lax.axis_index("prompt")
    c = lax.axis_index("comp")
    z = p // 2
    k = p % 2
    other = 1 - k
    group_col = c // 2
    group_row = p // 2
    kk = c // 8

    def ds(start, size):
        return pl.ds(pl.multiple_of(start, size), size)

    def local(src, dst, sem):
        copy = pltpu.make_async_copy(src, dst, lsem.at[sem])
        copy.start()
        return copy

    def remote(src, dst, send, recv, row, col):
        return pltpu.make_async_remote_copy(
            src_ref=src, dst_ref=dst, send_sem=ssem.at[send], recv_sem=rsem.at[recv],
            device_id=(row, col), device_id_type=MESH,
        )

    def arrived(dst, recv):
        remote(dst, dst, 0, recv, p, c).wait_recv()

    def sent(src, send):
        remote(src, src, send, 0, p, c).wait_send()

    b_col = group_col * STATE_WIDTH
    b_row = group_row * STATE_WIDTH
    copies = {}
    copies[L_PS] = local(pstep.at[ds(8 * k, 8), :], ps.at[k], L_PS)
    copies[L_PX] = local(inner.at[:, ds(k * HALF, HALF)], px.at[k], L_PX)
    copies[L_PB] = local(proj.at[:, ds(b_col, STATE_WIDTH)], pb.at[k], L_PB)
    copies[L_WX] = local(cvi.at[:, ds(c * FEAT + k * HALF, HALF)], wx, L_WX)
    copies[L_WB] = local(cvp.at[:, ds(b_col, STATE_WIDTH)], wb, L_WB)
    copies[L_SS] = local(sstep, ss, L_SS)
    copies[L_CG] = local(gate, cg, L_CG)
    copies[L_CX] = local(cin, cx, L_CX)
    copies[L_CB] = local(cproj.at[:, :, ds(b_row, STATE_WIDTH)], cbc.at[0], L_CB)
    copies[L_CC] = local(cproj.at[:, :, ds(PROJ_C + b_row, STATE_WIDTH)], cbc.at[1], L_CC)
    copies[L_WCX] = local(cvi.at[:, ds(p * FEAT, FEAT)], wcx, L_WCX)
    copies[L_WCB] = local(cvp.at[:, ds(b_row, STATE_WIDTH)], wcbc.at[0], L_WCB)
    copies[L_WCC] = local(cvp.at[:, ds(PROJ_C + b_row, STATE_WIDTH)], wcbc.at[1], L_WCC)

    barrier = pltpu.get_barrier_semaphore()

    def greet(row, col):
        pl.semaphore_signal(barrier, inc=1, device_id=(row, col), device_id_type=MESH)

    tail_self = jnp.logical_and(p == ROWS - 1, c == COLS - 1)
    red_self = jnp.logical_and(p == c, kk == k)
    greet(p + 1 - 2 * k, c)

    @pl.when(z > 0)
    def _():
        greet(2 * z - 1, c)

    for chip in range(CHIPS):
        @pl.when(jnp.logical_not(jnp.logical_and(red_self, z == chip)))
        def _():
            greet(2 * chip + kk, p)

    for step in range(1, COLS):
        greet(p, lax.rem(c + step, COLS))

    @pl.when(jnp.logical_not(tail_self))
    def _():
        greet(ROWS - 1, p)

    @pl.when(p < ROWS - 1)
    def _():
        greet(ROWS - 1, c)

    last_row = (p == ROWS - 1).astype(jnp.int32)
    halo_out = jnp.logical_and(k == 1, p < ROWS - 1)
    expected = (
        1 + 2 * halo_out.astype(jnp.int32) + CHIPS - red_self.astype(jnp.int32) + COLS - 1
        + last_row * (COLS + ROWS - 1) - tail_self.astype(jnp.int32)
    )
    pl.semaphore_wait(barrier, expected)

    sib = p + 1 - 2 * k
    sib_copies = [
        remote(pstep.at[ds(8 * other, 8), :], ps.at[k], S_SIB, R_SIB, sib, c),
        remote(inner.at[:, ds(other * HALF, HALF)], px.at[k], S_SIB + 1, R_SIB + 1, sib, c),
        remote(proj.at[:, ds(b_col, STATE_WIDTH)], pb.at[k], S_SIB + 2, R_SIB + 2, sib, c),
    ]

    def halo_copies():
        found = []
        for core in range(2):
            found.append(
                remote(
                    inner.at[pl.ds(TOK - 16, 16), pl.ds(core * HALF, HALF)], hx,
                    S_HALO + 2 * core, R_HALO, p + 1 + core, c,
                )
            )
            found.append(
                remote(
                    proj.at[pl.ds(TOK - 16, 16), ds(b_col, STATE_WIDTH)], hb,
                    S_HALO + 2 * core + 1, R_HALO + 1, p + 1 + core, c,
                )
            )
        return found

    @pl.when(halo_out)
    def _():
        for copy in halo_copies():
            copy.start()

    for copy in sib_copies:
        copy.start()

    @pl.when(z == 0)
    def _():
        hx[...] = jnp.zeros_like(hx)
        hb[...] = jnp.zeros_like(hb)

    tail_rows = pl.ds(TOK - 16, 16)

    def tail_inner(j):
        return remote(inner.at[tail_rows, :], tx, S_TX + j, R_TAIL, c, j)

    def tail_b(j):
        cols = ds((j // 2) * STATE_WIDTH, STATE_WIDTH)
        return remote(proj.at[tail_rows, cols], tbc.at[0], S_TB + j, R_TAIL + 1, j, c)

    def tail_c(j):
        cols = ds(PROJ_C + (j // 2) * STATE_WIDTH, STATE_WIDTH)
        return remote(proj.at[tail_rows, cols], tbc.at[1], S_TC + j, R_TAIL + 2, j, c)

    @pl.when(p == ROWS - 1)
    def _():
        for j in range(COLS):
            @pl.when(jnp.logical_not(jnp.logical_and(c == COLS - 1, j == COLS - 1)))
            def _():
                tail_inner(j).start()

        @pl.when(c == COLS - 1)
        def _():
            local(inner.at[tail_rows, :], tx, L_TX)

        for j in range(ROWS - 1):
            tail_b(j).start()
            tail_c(j).start()
        local(proj.at[tail_rows, ds(b_row, STATE_WIDTH)], tbc.at[0], L_TB)
        local(proj.at[tail_rows, ds(PROJ_C + b_row, STATE_WIDTH)], tbc.at[1], L_TC)

    row_id = lax.broadcasted_iota(jnp.int32, (TOK, TOK), 0)
    col_id = lax.broadcasted_iota(jnp.int32, (TOK, TOK), 1)
    tri = jnp.where(col_id <= row_id, 1.0, 0.0).astype(BF16)

    def running(values):
        a, b, d = split3(values)
        return dot_nt(a, tri) + (dot_nt(b, tri) + dot_nt(d, tri))

    def running_t(values):
        a, b, d = split3(values)
        return dot_nt(tri, a) + (dot_nt(tri, b) + dot_nt(tri, d))

    copies[L_SS].wait()
    rate_row = jnp.exp(pick_rows(dlog[...], p * 16, 16)) * LOG2E
    log_step = []
    raw = []
    for slot in range(2):
        dt = softplus(ss[:, slot, :])
        raw.append(-rate_row * dt)
        log_step.append(jnp.log2(dt))
    raw = jnp.concatenate(raw, axis=0)
    cum = running(raw)
    cum_t = running_t(raw)
    shifted = cum - jnp.concatenate(log_step, axis=0)

    copies[L_PS].wait()
    arrived(ps.at[other], R_SIB)
    rate_col = jnp.exp(pick_rows(dlog[...], c * 16 + 8 * k, 8)) * LOG2E
    dts = [softplus(ps[block]) for block in range(2)]
    cums = running(jnp.concatenate([-rate_col * dt for dt in dts], axis=0))
    cum0, cum1 = cums[:8], cums[8:]
    tot0, tot1 = cum0[:, TOK - 1 :], cum1[:, TOK - 1 :]
    weights = [jnp.exp2(tot0 - cum0 + tot1) * dts[0], jnp.exp2(tot1 - cum1) * dts[1]]
    total = jnp.broadcast_to(tot0 + tot1, (8, 128))
    for i in range(8):
        logs[i] = jnp.broadcast_to(total[i : i + 1], (8, 128))

    def red_dest(i):
        return 8 * k + i

    def own(i):
        return jnp.logical_and(p == c, red_dest(i) == c)

    def log_copy(i):
        return remote(logs.at[i], redlog.at[z], S_LOG + i, R_LOG + z, c, red_dest(i))

    def red_copy(i):
        return remote(
            st.at[pl.ds(i * HEAD_WIDTH, HEAD_WIDTH), :], red.at[z], S_RED + i, R_RED + z, c, red_dest(i)
        )

    for i in range(8):
        @pl.when(jnp.logical_not(own(i)))
        def _():
            log_copy(i).start()

        @pl.when(own(i))
        def _():
            redlog[z] = logs[i]

    spread = jnp.where(
        lax.broadcasted_iota(jnp.int32, (8, HALF), 1) // HEAD_WIDTH
        == lax.broadcasted_iota(jnp.int32, (8, HALF), 0),
        1.0,
        0.0,
    ).astype(BF16)
    spread3 = jnp.concatenate([spread.astype(F32)] * 3, axis=0).astype(BF16)
    weights3 = [
        jnp.concatenate([part_.astype(F32) for part_ in split3(w)], axis=0).astype(BF16) for w in weights
    ]

    copies[L_PB].wait()
    copies[L_WB].wait()
    copies[L_PX].wait()
    copies[L_WX].wait()

    @pl.when(z > 0)
    def _():
        arrived(hx, R_HALO)
        arrived(hb, R_HALO + 1)

    arrived(pb.at[other], R_SIB + 2)
    arrived(px.at[other], R_SIB + 1)

    taps_b = wb[...].astype(F32)
    bb = [
        causal_conv(pb[0], hb[...], taps_b).astype(BF16),
        causal_conv(pb[1], pb[0, pl.ds(TOK - 16, 16), :], taps_b).astype(BF16),
    ]
    for pair in range(4):
        cols = pl.ds(pair * 128, 128)
        taps = wx[:, cols].astype(F32)
        acc = None
        for block in range(2):
            lead = hx[:, cols] if block == 0 else px[0, pl.ds(TOK - 16, 16), cols]
            x = causal_conv(px[block, :, cols], lead, taps)
            wide = dot_tn(weights3[block], spread3[:, pair * 128 : pair * 128 + 128])
            made = dot_tn((x * wide).astype(BF16), bb[block])
            acc = made if acc is None else acc + made
        st[pl.ds(pair * 128, 128), :] = acc.astype(BF16)
        for i in (2 * pair, 2 * pair + 1):
            @pl.when(jnp.logical_not(own(i)))
            def _():
                red_copy(i).start()

            @pl.when(own(i))
            def _():
                red[z] = st[pl.ds(i * HEAD_WIDTH, HEAD_WIDTH), :]

    copies[L_CB].wait()
    copies[L_CC].wait()
    copies[L_WCB].wait()
    copies[L_WCC].wait()
    copies[L_WCX].wait()
    copies[L_CX].wait()
    copies[L_CG].wait()

    @pl.when(jnp.logical_not(tail_self))
    def _():
        arrived(tx, R_TAIL)

    @pl.when(tail_self)
    def _():
        pltpu.make_async_copy(inner.at[tail_rows, :], tx, lsem.at[L_TX]).wait()

    @pl.when(p < ROWS - 1)
    def _():
        arrived(tbc.at[0], R_TAIL + 1)
        arrived(tbc.at[1], R_TAIL + 2)

    @pl.when(p == ROWS - 1)
    def _():
        pltpu.make_async_copy(proj.at[tail_rows, ds(b_row, STATE_WIDTH)], tbc.at[0], lsem.at[L_TB]).wait()
        pltpu.make_async_copy(proj.at[tail_rows, ds(b_row, STATE_WIDTH)], tbc.at[1], lsem.at[L_TC]).wait()

    for slot in range(2):
        for which in range(2):
            bcv[which, slot] = causal_conv(
                cbc[which, slot], tbc[which], wcbc[which].astype(F32)
            ).astype(BF16)
        scores[slot] = dot_nt(bcv[1, slot], bcv[0, slot])

    lane_low = lax.broadcasted_iota(jnp.int32, (TOK, 128), 1) < HEAD_WIDTH
    causal = (
        lax.broadcasted_iota(jnp.int32, (128, 128), 1) <= lax.broadcasted_iota(jnp.int32, (128, 128), 0)
    )

    def intra(slot, pair):
        cols = pl.ds(pair * 128, 128)
        x = causal_conv(cx[slot, :, cols], tx[:, cols], wcx[:, cols].astype(F32)).astype(BF16)
        made = []
        spread_logs = []
        for h in (2 * pair, 2 * pair + 1):
            at = slot * 16 + h
            down = jnp.broadcast_to(cum_t[:, at : at + 1], (TOK, 128))
            left = down - shifted[at : at + 1, :128]
            right = down[128:] - shifted[at : at + 1, 128:]
            top = jnp.exp2(jnp.where(causal, left[:128], -jnp.inf)) * scores[slot, :128, :128]
            low = jnp.exp2(left[128:]) * scores[slot, 128:, :128]
            diag = jnp.exp2(jnp.where(causal, right, -jnp.inf)) * scores[slot, 128:, 128:]
            y0 = jnp.dot(top.astype(BF16), x[:128], preferred_element_type=F32)
            y1 = jnp.dot(low.astype(BF16), x[:128], preferred_element_type=F32) + jnp.dot(
                diag.astype(BF16), x[128:], preferred_element_type=F32
            )
            made.append(jnp.concatenate([y0, y1], axis=0))
            spread_logs.append(down)
        g = silu(cg[slot, :, cols].astype(F32))
        part[slot, :, cols] = jnp.where(lane_low, made[0], made[1]) * g
        coef[slot, :, cols] = jnp.exp2(jnp.where(lane_low, spread_logs[0], spread_logs[1])) * g

    work = [(slot, pair) for slot in range(2) for pair in range(8)]
    for slot, pair in work[:10]:
        intra(slot, pair)

    for chip in range(CHIPS):
        @pl.when(jnp.logical_not(jnp.logical_and(red_self, z == chip)))
        def _():
            arrived(redlog.at[chip], R_LOG + chip)
            arrived(red.at[chip], R_RED + chip)

    later = jnp.zeros((8, 128), F32)
    state = None
    for chip in range(CHIPS - 1, -1, -1):
        scale = jnp.exp2(later)[:1, :1]
        term = red[chip].astype(F32) * scale
        state = term if state is None else state + term
        later = later + redlog[chip]
    mine = ds(c * HEAD_WIDTH, HEAD_WIDTH)
    stf[mine, :] = state.astype(BF16)

    def ag_copy(step):
        return remote(stf.at[mine, :], stf.at[mine, :], S_AG + step - 1, R_AG + c, p, lax.rem(c + step, COLS))

    for step in range(1, COLS):
        ag_copy(step).start()

    for slot, pair in work[10:]:
        intra(slot, pair)

    for step in range(1, COLS):
        source = lax.rem(c + step, COLS)
        arrived(stf.at[ds(source * HEAD_WIDTH, HEAD_WIDTH), :], R_AG + source)

    def sq_copy(slot):
        return remote(sq.at[slot], sqs.at[slot], S_SQ + slot, R_SQ + slot, sib, c)

    for slot in range(2):
        squares = jnp.zeros((TOK, 128), F32)
        for chunk in range(4):
            cols = pl.ds(chunk * 256, 256)
            read = dot_nt(bcv[1, slot], stf[cols, :])
            gated = part[slot, :, cols] + coef[slot, :, cols] * read
            part[slot, :, cols] = gated
            squares = squares + gated[:, :128] * gated[:, :128] + gated[:, 128:] * gated[:, 128:]
        sq[slot] = squares
        sq_copy(slot).start()

    gains = gain[...]
    position = lax.broadcasted_iota(jnp.int32, (TOK, 1), 0)
    outs = []
    for slot in range(2):
        arrived(sqs.at[slot], R_SQ + slot)
        mean = jnp.sum(sq[slot] + sqs[slot], axis=1, keepdims=True) * (1.0 / (GROUP_HEADS * HEAD_WIDTH))
        scale = jnp.where(position < slen[slot], lax.rsqrt(mean + EPS), 0.0)
        obuf[slot] = (part[slot] * scale * gains).astype(BF16)
        copy = pltpu.make_async_copy(obuf.at[slot], out.at[slot], lsem.at[L_OUT + slot])
        copy.start()
        outs.append(copy)

    for copy in sib_copies:
        copy.wait_send()

    @pl.when(halo_out)
    def _():
        for copy in halo_copies():
            copy.wait_send()

    @pl.when(p == ROWS - 1)
    def _():
        for j in range(COLS):
            @pl.when(jnp.logical_not(jnp.logical_and(c == COLS - 1, j == COLS - 1)))
            def _():
                tail_inner(j).wait_send()
        for j in range(ROWS - 1):
            tail_b(j).wait_send()
            tail_c(j).wait_send()

    for i in range(8):
        @pl.when(jnp.logical_not(own(i)))
        def _():
            log_copy(i).wait_send()
            red_copy(i).wait_send()

    for step in range(1, COLS):
        ag_copy(step).wait_send()
    for slot in range(2):
        sq_copy(slot).wait_send()
    for copy in outs:
        copy.wait()


def local(
    prompt_inner,
    prompt_proj,
    prompt_step,
    completion_inner,
    completion_gate,
    completion_projections,
    sample_step,
    sample_length,
    decay_log,
    conv_inner,
    conv_proj,
    norm_gain,
):
    hbm = pl.BlockSpec(memory_space=pl.ANY)
    vmem = pl.BlockSpec(memory_space=pltpu.VMEM)
    smem = pl.BlockSpec(memory_space=pltpu.SMEM)
    V = pltpu.VMEM
    return pl.pallas_call(
        kernel,
        out_shape=jax.ShapeDtypeStruct(completion_inner.shape, BF16),
        in_specs=[hbm, hbm, hbm, hbm, hbm, hbm, hbm, smem, vmem, hbm, hbm, vmem],
        out_specs=hbm,
        scratch_shapes=[
            V((2, TOK, HALF), BF16),
            V((2, TOK, STATE_WIDTH), BF16),
            V((2, 8, TOK), F32),
            V((16, HALF), BF16),
            V((16, STATE_WIDTH), BF16),
            V((CONV, HALF), BF16),
            V((CONV, STATE_WIDTH), BF16),
            V((2, TOK, FEAT), BF16),
            V((2, TOK, FEAT), BF16),
            V((2, 2, TOK, STATE_WIDTH), BF16),
            V((16, 2, TOK), F32),
            V((CONV, FEAT), BF16),
            V((2, CONV, STATE_WIDTH), BF16),
            V((16, FEAT), BF16),
            V((2, 16, STATE_WIDTH), BF16),
            V((HALF, STATE_WIDTH), BF16),
            V((8, 8, 128), F32),
            V((CHIPS, HEAD_WIDTH, STATE_WIDTH), BF16),
            V((CHIPS, 8, 128), F32),
            V((FEAT, STATE_WIDTH), BF16),
            V((8, 128), BF16),
            V((2, 2, TOK, STATE_WIDTH), BF16),
            V((2, TOK, FEAT), F32),
            V((2, TOK, FEAT), F32),
            V((2, TOK, TOK), F32),
            V((2, TOK, 128), F32),
            V((2, TOK, 128), F32),
            V((2, TOK, FEAT), BF16),
            pltpu.SemaphoreType.DMA((N_LOCAL,)),
            pltpu.SemaphoreType.DMA((N_SEND,)),
            pltpu.SemaphoreType.DMA((N_RECV,)),
        ],
        compiler_params=pltpu.CompilerParams(
            collective_id=0, has_side_effects=True, vmem_limit_bytes=48 << 20
        ),
        name="layer",
    )(
        prompt_inner,
        prompt_proj,
        prompt_step,
        completion_inner,
        completion_gate,
        completion_projections,
        sample_step,
        sample_length,
        decay_log.reshape(1, STATE_HEADS),
        conv_inner,
        conv_proj,
        norm_gain.reshape(1, FEAT),
    )


def solution(mesh):
    placed = (
        P("prompt", "comp"),
        P("prompt", None),
        P("comp", "prompt"),
        P("comp", None, "prompt"),
        P("comp", None, "prompt"),
        P("comp", None, None),
        P("prompt", "comp", None),
        P("comp"),
        P(),
        P(),
        P(),
        P("prompt"),
    )
    return jax.shard_map(
        local, mesh=mesh, in_specs=placed, out_specs=P("comp", None, "prompt"), check_vma=False
    )
```

```python
import functools

import jax
import jax.numpy as jnp
from jax import lax
from jax.experimental import pallas as pl
from jax.experimental.pallas import tpu as pltpu
from jax.sharding import PartitionSpec as P

STATE_HEADS = 256
HEAD_WIDTH = 64
STATE_WIDTH = 256
STATE_GROUPS = 8
CONV = 4
EPS = 1e-05
LOG2E = 1.4426950408889634

MESH = pl.DeviceIdType.MESH
F32 = jnp.float32
BF16 = jnp.bfloat16

ROWS = 16
COLS = 16
CHIPS = 8
TOK = 256
FEAT = 1024
HALF = 512
GROUP_HEADS = 32
PROJ_C = STATE_GROUPS * STATE_WIDTH

EDGE = 8
HALVES = 2
PIECE = HEAD_WIDTH // HALVES

R_SIB, R_HALO, R_TAIL, R_LOG, R_MID = 0, 3, 5, 8, 16
R_RED = R_MID + CHIPS * HALVES
R_AG = R_RED + CHIPS * HALVES
R_SQ = R_AG + COLS * HALVES
N_RECV = R_SQ + 2
S_SIB, S_HALO, S_TX, S_RELAY, S_TB = 0, 3, 7, 8, 23
S_TC = S_TB + 15
S_LOG = S_TC + 15
S_MID = S_LOG + 8
S_RED = S_MID + CHIPS * HALVES
S_AG = S_RED + CHIPS * HALVES
S_SQ = S_AG + (COLS - 1) * HALVES
N_SEND = S_SQ + 2
(L_PX, L_PB, L_PS, L_WX, L_WB, L_CX, L_CG, L_CB, L_CC, L_SS, L_WCX, L_WCB, L_WCC, L_TX, L_TB, L_TC, L_OUT) = range(17)
N_LOCAL = 18


def silu(v):
    h = 0.5 * v
    return h + h * jnp.tanh(h)


def softplus(v):
    return jnp.maximum(v, 0.0) + jnp.log1p(jnp.exp(-jnp.abs(v)))


def split3(v):
    a = v.astype(BF16)
    r = v - a.astype(F32)
    b = r.astype(BF16)
    c = (r - b.astype(F32)).astype(BF16)
    return a, b, c


def dot_nt(a, b):
    return lax.dot_general(a, b, (((1,), (1,)), ((), ())), preferred_element_type=F32)


def dot_tn(a, b):
    return lax.dot_general(a, b, (((0,), (0,)), ((), ())), preferred_element_type=F32)


def convolve(x, taps):
    total = x * taps[3:4]
    for lag in (1, 2, 3):
        total = total + pltpu.roll(x, lag, 0) * taps[3 - lag : 4 - lag]
    return silu(total)


def causal_conv(src, lead, taps):
    return convolve(jnp.concatenate([lead.astype(F32), src.astype(F32)], axis=0), taps)[EDGE:]


def pick_rows(row, first, count):
    lanes = lax.broadcasted_iota(jnp.int32, (count, row.shape[1]), 1)
    heads = first + lax.broadcasted_iota(jnp.int32, (count, row.shape[1]), 0)
    wide = jnp.broadcast_to(row, (count, row.shape[1]))
    return jnp.sum(jnp.where(lanes == heads, wide, 0.0), axis=1, keepdims=True)


def kernel(
    inner, proj, pstep, cin, gate, cproj, sstep, slen, dlog, cvi, cvp, gain, out,
    px, pb, ps, hx, hb, wx, wb, cx, cg, cbc, ss, wcx, wcbc, tx, tbc,
    xw, wide, bb, st, logs, redlog, mid, red, stf, xcv, bcv, part, coef, scores, sq, sqs, obuf,
    lsem, ssem, rsem,
):
    p = lax.axis_index("prompt")
    c = lax.axis_index("comp")
    z = p // 2
    k = p % 2
    other = 1 - k
    sib = p + 1 - 2 * k
    group_col = c // 2
    group_row = p // 2
    kk = c // 8
    c_core = c % 2
    no = jnp.logical_not
    both = jnp.logical_and

    def ds(start, size):
        return pl.ds(pl.multiple_of(start, size), size)

    def local(src, dst, sem):
        copy = pltpu.make_async_copy(src, dst, lsem.at[sem])
        copy.start()
        return copy

    def remote(src, dst, send, recv, row, col):
        return pltpu.make_async_remote_copy(
            src_ref=src, dst_ref=dst, send_sem=ssem.at[send], recv_sem=rsem.at[recv],
            device_id=(row, col), device_id_type=MESH,
        )

    def arrived(dst, recv):
        remote(dst, dst, 0, recv, p, c).wait_recv()

    barrier = pltpu.get_barrier_semaphore()

    def greet(row, col):
        pl.semaphore_signal(barrier, inc=1, device_id=(row, col), device_id_type=MESH)

    tail_self = both(p == ROWS - 1, c == COLS - 1)
    log_self = both(p == c, kk == k)
    mid_self = both(kk == k, c_core == k)
    greet(sib, c)

    @pl.when(z > 0)
    def _():
        greet(2 * z - 1, c)

    for j in range(CHIPS):
        @pl.when(no(both(mid_self, c // 2 == j)))
        def _():
            greet(2 * z + kk, 2 * j + k)

    for step in range(1, CHIPS):
        greet(lax.rem(p + 2 * step, ROWS), c)

    for step in range(1, COLS):
        greet(p, lax.rem(c + step, COLS))

    for chip in range(CHIPS):
        @pl.when(no(both(log_self, z == chip)))
        def _():
            greet(2 * chip + kk, p)

    @pl.when(both(p == c, p < ROWS - 1))
    def _():
        greet(ROWS - 1, c)

    @pl.when(p < ROWS - 1)
    def _():
        greet(ROWS - 1, c)

    b_col = group_col * STATE_WIDTH
    b_row = group_row * STATE_WIDTH
    copies = {}
    copies[L_PS] = local(pstep.at[ds(8 * k, 8), :], ps.at[k], L_PS)
    copies[L_PB] = local(proj.at[:, ds(b_col, STATE_WIDTH)], pb.at[k], L_PB)
    copies[L_WB] = local(cvp.at[:, ds(b_col, STATE_WIDTH)], wb, L_WB)
    copies[L_PX] = local(inner.at[:, ds(k * HALF, HALF)], px.at[k], L_PX)
    copies[L_WX] = local(cvi.at[:, ds(c * FEAT + k * HALF, HALF)], wx, L_WX)

    last_row = (p == ROWS - 1).astype(jnp.int32)
    halo_out = both(k == 1, p < ROWS - 1)
    expected = (
        1 + 2 * halo_out.astype(jnp.int32)
        + CHIPS - mid_self.astype(jnp.int32) + CHIPS - 1 + COLS - 1 + CHIPS - log_self.astype(jnp.int32)
        + last_row * ROWS - tail_self.astype(jnp.int32)
    )
    pl.semaphore_wait(barrier, expected)

    edge_rows = pl.ds(TOK - EDGE, EDGE)
    sib_copies = [
        remote(pstep.at[ds(8 * other, 8), :], ps.at[k], S_SIB, R_SIB, sib, c),
        remote(proj.at[:, ds(b_col, STATE_WIDTH)], pb.at[k], S_SIB + 1, R_SIB + 1, sib, c),
        remote(inner.at[:, ds(other * HALF, HALF)], px.at[k], S_SIB + 2, R_SIB + 2, sib, c),
    ]

    def halo_copies():
        found = []
        for core in range(2):
            found.append(
                remote(
                    inner.at[edge_rows, pl.ds(core * HALF, HALF)], hx,
                    S_HALO + 2 * core, R_HALO, p + 1 + core, c,
                )
            )
            found.append(
                remote(
                    proj.at[edge_rows, ds(b_col, STATE_WIDTH)], hb,
                    S_HALO + 2 * core + 1, R_HALO + 1, p + 1 + core, c,
                )
            )
        return found

    @pl.when(halo_out)
    def _():
        for copy in halo_copies():
            copy.start()

    for copy in sib_copies:
        copy.start()

    @pl.when(z == 0)
    def _():
        hx[...] = jnp.zeros_like(hx)
        hb[...] = jnp.zeros_like(hb)

    def tail_copy():
        return remote(inner.at[edge_rows, :], tx, S_TX, R_TAIL, c, c)

    def relay_copy(step):
        return remote(tx, tx, S_RELAY + step - 1, R_TAIL, p, lax.rem(c + step, COLS))

    def tail_b(j):
        cols = ds((j // 2) * STATE_WIDTH, STATE_WIDTH)
        return remote(proj.at[edge_rows, cols], tbc.at[0], S_TB + j, R_TAIL + 1, j, c)

    def tail_c(j):
        cols = ds(PROJ_C + (j // 2) * STATE_WIDTH, STATE_WIDTH)
        return remote(proj.at[edge_rows, cols], tbc.at[1], S_TC + j, R_TAIL + 2, j, c)

    def tail_local():
        return pltpu.make_async_copy(inner.at[edge_rows, :], tx, lsem.at[L_TX])

    def tail_local_b():
        return pltpu.make_async_copy(proj.at[edge_rows, ds(b_row, STATE_WIDTH)], tbc.at[0], lsem.at[L_TB])

    def tail_local_c():
        return pltpu.make_async_copy(
            proj.at[edge_rows, ds(PROJ_C + b_row, STATE_WIDTH)], tbc.at[1], lsem.at[L_TC]
        )

    tail_out = both(p == ROWS - 1, c < COLS - 1)

    @pl.when(tail_out)
    def _():
        tail_copy().start()

    @pl.when(tail_self)
    def _():
        tail_local().start()

    copies[L_SS] = local(sstep, ss, L_SS)
    copies[L_CX] = local(cin, cx, L_CX)
    copies[L_WCX] = local(cvi.at[:, ds(p * FEAT, FEAT)], wcx, L_WCX)
    copies[L_CB] = local(cproj.at[:, :, ds(b_row, STATE_WIDTH)], cbc.at[0], L_CB)
    copies[L_CC] = local(cproj.at[:, :, ds(PROJ_C + b_row, STATE_WIDTH)], cbc.at[1], L_CC)
    copies[L_WCB] = local(cvp.at[:, ds(b_row, STATE_WIDTH)], wcbc.at[0], L_WCB)
    copies[L_WCC] = local(cvp.at[:, ds(PROJ_C + b_row, STATE_WIDTH)], wcbc.at[1], L_WCC)
    copies[L_CG] = local(gate, cg, L_CG)

    row_id = lax.broadcasted_iota(jnp.int32, (TOK, TOK), 0)
    col_id = lax.broadcasted_iota(jnp.int32, (TOK, TOK), 1)
    tri = jnp.where(col_id <= row_id, 1.0, 0.0).astype(BF16)

    def running(values):
        a, b, d = split3(values)
        return dot_nt(a, tri) + (dot_nt(b, tri) + dot_nt(d, tri))

    def running_t(values):
        a, b, d = split3(values)
        return dot_nt(tri, a) + (dot_nt(tri, b) + dot_nt(tri, d))

    rate_col = jnp.exp(pick_rows(dlog[...], c * 16 + 8 * k, 8)) * LOG2E
    spread = jnp.where(
        lax.broadcasted_iota(jnp.int32, (24, HALF), 1) // HEAD_WIDTH
        == lax.broadcasted_iota(jnp.int32, (24, HALF), 0) % 8,
        1.0,
        0.0,
    ).astype(BF16)

    def weigh(block):
        dt = softplus(ps[block])
        run = running(-rate_col * dt)
        total = run[:, TOK - 1 :]
        weight = jnp.exp2(total - run) * dt
        pieces = jnp.concatenate([piece.astype(F32) for piece in split3(weight)], axis=0).astype(BF16)
        wide[block] = dot_tn(pieces, spread)
        return total

    def conv_b(block):
        x = pb[block].astype(F32)
        bb[block] = convolve(x, wb[...].astype(F32)).astype(BF16)

    def conv_x(block):
        for quarter in range(4):
            cols = pl.ds(quarter * 128, 128)
            x = px[block, :, cols].astype(F32)
            xw[block, :, cols] = (convolve(x, wx[:, cols].astype(F32)) * wide[block, :, cols]).astype(BF16)

    copies[L_PS].wait()
    total_own = weigh(k)
    copies[L_PB].wait()
    copies[L_WB].wait()
    conv_b(k)
    copies[L_PX].wait()
    copies[L_WX].wait()
    conv_x(k)
    arrived(ps.at[other], R_SIB)
    total_sib = weigh(other)
    total1 = jnp.where(k == 1, total_own, total_sib)
    total_chip = jnp.broadcast_to(total_own + total_sib, (8, 128))
    for i in range(8):
        logs[i] = total_chip[i : i + 1]

    def log_dest(i):
        return 8 * k + i

    def log_own(i):
        return both(p == c, log_dest(i) == c)

    def log_copy(i):
        return remote(logs.at[i], redlog.at[z], S_LOG + i, R_LOG + z, c, log_dest(i))

    for i in range(8):
        @pl.when(no(log_own(i)))
        def _():
            log_copy(i).start()

        @pl.when(log_own(i))
        def _():
            redlog[z] = logs[i]

    arrived(pb.at[other], R_SIB + 1)
    conv_b(other)
    arrived(px.at[other], R_SIB + 2)
    conv_x(other)

    @pl.when(z > 0)
    def _():
        arrived(hx, R_HALO)
        arrived(hb, R_HALO + 1)

    for block in range(2):
        lead_b = hb[...] if block == 0 else pb[0, edge_rows, :]
        lead_x = hx[...] if block == 0 else px[0, edge_rows, :]
        bb[block, :16, :] = causal_conv(pb[block, :16, :], lead_b, wb[...].astype(F32)).astype(BF16)
        xw[block, :16, :] = (
            causal_conv(px[block, :16, :], lead_x, wx[...].astype(F32)) * wide[block, :16, :]
        ).astype(BF16)

    def mid_copy(i, half):
        rows = pl.ds(i * HEAD_WIDTH + half * PIECE, PIECE)
        return remote(
            st.at[rows, :], mid.at[c // 2, pl.ds(half * PIECE, PIECE), :],
            S_MID + 2 * i + half, R_MID + 2 * (c // 2) + half, 2 * z + c_core, 8 * k + i,
        )

    def mid_own(i):
        return both(mid_self, 8 * k + i == c)

    decay1 = jnp.exp2(jnp.broadcast_to(total1, (8, STATE_WIDTH)))
    for pair in range(4):
        cols = pl.ds(pair * 128, 128)
        first = dot_tn(xw[0, :, cols], bb[0])
        second = dot_tn(xw[1, :, cols], bb[1])
        for side in range(2):
            i = 2 * pair + side
            rows = slice(side * HEAD_WIDTH, (side + 1) * HEAD_WIDTH)
            st[pl.ds(i * HEAD_WIDTH, HEAD_WIDTH), :] = (
                first[rows] * decay1[i : i + 1] + second[rows]
            ).astype(BF16)

            @pl.when(no(mid_own(i)))
            def _():
                for half in range(HALVES):
                    mid_copy(i, half).start()

            @pl.when(mid_own(i))
            def _():
                mid[c // 2] = st[pl.ds(i * HEAD_WIDTH, HEAD_WIDTH), :]

    @pl.when(p == ROWS - 1)
    def _():
        for j in range(ROWS - 1):
            tail_b(j).start()
            tail_c(j).start()
        tail_local_b().start()
        tail_local_c().start()

    @pl.when(both(p == c, no(tail_self)))
    def _():
        arrived(tx, R_TAIL)

    @pl.when(tail_self)
    def _():
        tail_local().wait()

    @pl.when(p == c)
    def _():
        for step in range(1, COLS):
            relay_copy(step).start()

    copies[L_CB].wait()
    copies[L_CC].wait()
    copies[L_WCB].wait()
    copies[L_WCC].wait()
    copies[L_WCX].wait()
    copies[L_CX].wait()
    copies[L_CG].wait()
    for slot in range(2):
        for eighth in range(8):
            cols = pl.ds(eighth * 128, 128)
            x = cx[slot, :, cols].astype(F32)
            xcv[slot, :, cols] = convolve(x, wcx[:, cols].astype(F32)).astype(BF16)
        for which in range(2):
            x = cbc[which, slot].astype(F32)
            bcv[which, slot] = convolve(x, wcbc[which].astype(F32)).astype(BF16)

    copies[L_SS].wait()
    rate_row = jnp.exp(pick_rows(dlog[...], p * 16, 16)) * LOG2E
    log_step = []
    raw = []
    for slot in range(2):
        dt = softplus(ss[:, slot, :])
        raw.append(-rate_row * dt)
        log_step.append(jnp.log2(dt))
    raw = jnp.concatenate(raw, axis=0)
    cum = running(raw)
    cum_t = running_t(raw)
    shifted = cum - jnp.concatenate(log_step, axis=0)

    def red_copy(j, half):
        rows = pl.ds(half * PIECE, PIECE)
        return remote(
            mid.at[j, rows, :], red.at[z, rows, :],
            S_RED + 2 * j + half, R_RED + 2 * z + half, 2 * j + k, c,
        )

    for half in range(HALVES):
        rows = pl.ds(half * PIECE, PIECE)
        for j in range(CHIPS):
            @pl.when(no(both(mid_self, c // 2 == j)))
            def _():
                arrived(mid.at[j, rows, :], R_MID + 2 * j + half)

            @pl.when(z != j)
            def _():
                red_copy(j, half).start()

            @pl.when(z == j)
            def _():
                red[z, rows, :] = mid[j, rows, :]

    @pl.when(p != c)
    def _():
        arrived(tx, R_TAIL)

    @pl.when(p < ROWS - 1)
    def _():
        arrived(tbc.at[0], R_TAIL + 1)
        arrived(tbc.at[1], R_TAIL + 2)

    @pl.when(p == ROWS - 1)
    def _():
        tail_local_b().wait()
        tail_local_c().wait()

    for slot in range(2):
        xcv[slot, :16, :] = causal_conv(cx[slot, :16, :], tx[...], wcx[...].astype(F32)).astype(BF16)
        for which in range(2):
            bcv[which, slot, :16, :] = causal_conv(
                cbc[which, slot, :16, :], tbc[which], wcbc[which].astype(F32)
            ).astype(BF16)
        scores[slot] = dot_nt(bcv[1, slot], bcv[0, slot])

    lane_low = lax.broadcasted_iota(jnp.int32, (TOK, 128), 1) < HEAD_WIDTH
    causal = (
        lax.broadcasted_iota(jnp.int32, (128, 128), 1) <= lax.broadcasted_iota(jnp.int32, (128, 128), 0)
    )

    def intra(slot, pair):
        cols = pl.ds(pair * 128, 128)
        x = xcv[slot, :, cols]
        made = []
        spread_logs = []
        for h in (2 * pair, 2 * pair + 1):
            at = slot * 16 + h
            down = jnp.broadcast_to(cum_t[:, at : at + 1], (TOK, 128))
            left = down - shifted[at : at + 1, :128]
            right = down[128:] - shifted[at : at + 1, 128:]
            top = jnp.exp2(jnp.where(causal, left[:128], -jnp.inf)) * scores[slot, :128, :128]
            low = jnp.exp2(left[128:]) * scores[slot, 128:, :128]
            diag = jnp.exp2(jnp.where(causal, right, -jnp.inf)) * scores[slot, 128:, 128:]
            y0 = jnp.dot(top.astype(BF16), x[:128], preferred_element_type=F32)
            y1 = jnp.dot(low.astype(BF16), x[:128], preferred_element_type=F32) + jnp.dot(
                diag.astype(BF16), x[128:], preferred_element_type=F32
            )
            made.append(jnp.concatenate([y0, y1], axis=0))
            spread_logs.append(down)
        g = silu(cg[slot, :, cols].astype(F32))
        part[slot, :, cols] = jnp.where(lane_low, made[0], made[1]) * g
        coef[slot, :, cols] = jnp.exp2(jnp.where(lane_low, spread_logs[0], spread_logs[1])) * g

    for slot in range(2):
        for pair in range(8):
            intra(slot, pair)

    for chip in range(CHIPS):
        @pl.when(no(both(log_self, z == chip)))
        def _():
            arrived(redlog.at[chip], R_LOG + chip)

    later = jnp.zeros((1, 128), F32)
    scales = []
    for chip in range(CHIPS - 1, -1, -1):
        scales.insert(0, jnp.exp2(later)[:, :1])
        later = later + redlog[chip]

    def mine(half):
        return ds(c * HEAD_WIDTH + half * PIECE, PIECE)

    def ag_copy(step, half):
        return remote(
            stf.at[mine(half), :], stf.at[mine(half), :],
            S_AG + HALVES * (step - 1) + half, R_AG + HALVES * c + half, p, lax.rem(c + step, COLS),
        )

    for half in range(HALVES):
        rows = pl.ds(half * PIECE, PIECE)
        for chip in range(CHIPS):
            @pl.when(z != chip)
            def _():
                arrived(red.at[chip, rows, :], R_RED + 2 * chip + half)

        state = None
        for chip in range(CHIPS):
            term = red[chip, rows, :].astype(F32) * scales[chip]
            state = term if state is None else state + term
        stf[mine(half), :] = state.astype(BF16)
        for step in range(1, COLS):
            ag_copy(step, half).start()

    def sq_copy(slot):
        return remote(sq.at[slot], sqs.at[slot], S_SQ + slot, R_SQ + slot, sib, c)

    for chunk in range(4):
        for source in range(4 * chunk, 4 * chunk + 4):
            @pl.when(c != source)
            def _():
                for half in range(HALVES):
                    arrived(
                        stf.at[pl.ds(source * HEAD_WIDTH + half * PIECE, PIECE), :],
                        R_AG + HALVES * source + half,
                    )

        cols = pl.ds(chunk * 256, 256)
        for slot in range(2):
            read = dot_nt(bcv[1, slot], stf[cols, :])
            gated = part[slot, :, cols] + coef[slot, :, cols] * read
            part[slot, :, cols] = gated
            squares = gated[:, :128] * gated[:, :128] + gated[:, 128:] * gated[:, 128:]
            sq[slot] = squares if chunk == 0 else sq[slot] + squares
            if chunk == 3:
                sq_copy(slot).start()

    gains = gain[...]
    position = lax.broadcasted_iota(jnp.int32, (TOK, 1), 0)
    outs = []
    for slot in range(2):
        arrived(sqs.at[slot], R_SQ + slot)
        mean = jnp.sum(sq[slot] + sqs[slot], axis=1, keepdims=True) * (1.0 / (GROUP_HEADS * HEAD_WIDTH))
        scale = jnp.where(position < slen[slot], lax.rsqrt(mean + EPS), 0.0)
        obuf[slot] = (part[slot] * scale * gains).astype(BF16)
        copy = pltpu.make_async_copy(obuf.at[slot], out.at[slot], lsem.at[L_OUT + slot])
        copy.start()
        outs.append(copy)

    for copy in sib_copies:
        copy.wait_send()

    @pl.when(halo_out)
    def _():
        for copy in halo_copies():
            copy.wait_send()

    @pl.when(tail_out)
    def _():
        tail_copy().wait_send()

    @pl.when(p == c)
    def _():
        for step in range(1, COLS):
            relay_copy(step).wait_send()

    @pl.when(p == ROWS - 1)
    def _():
        for j in range(ROWS - 1):
            tail_b(j).wait_send()
            tail_c(j).wait_send()

    for i in range(8):
        @pl.when(no(log_own(i)))
        def _():
            log_copy(i).wait_send()

        @pl.when(no(mid_own(i)))
        def _():
            for half in range(HALVES):
                mid_copy(i, half).wait_send()

    for half in range(HALVES):
        for j in range(CHIPS):
            @pl.when(z != j)
            def _():
                red_copy(j, half).wait_send()

        for step in range(1, COLS):
            ag_copy(step, half).wait_send()
    for slot in range(2):
        sq_copy(slot).wait_send()
    for copy in outs:
        copy.wait()


def local(
    prompt_inner,
    prompt_proj,
    prompt_step,
    completion_inner,
    completion_gate,
    completion_projections,
    sample_step,
    sample_length,
    decay_log,
    conv_inner,
    conv_proj,
    norm_gain,
):
    hbm = pl.BlockSpec(memory_space=pl.ANY)
    vmem = pl.BlockSpec(memory_space=pltpu.VMEM)
    smem = pl.BlockSpec(memory_space=pltpu.SMEM)
    V = pltpu.VMEM
    return pl.pallas_call(
        kernel,
        out_shape=jax.ShapeDtypeStruct(completion_inner.shape, BF16),
        in_specs=[hbm, hbm, hbm, hbm, hbm, hbm, hbm, smem, vmem, hbm, hbm, vmem],
        out_specs=hbm,
        scratch_shapes=[
            V((2, TOK, HALF), BF16),
            V((2, TOK, STATE_WIDTH), BF16),
            V((2, 8, TOK), F32),
            V((EDGE, HALF), BF16),
            V((EDGE, STATE_WIDTH), BF16),
            V((CONV, HALF), BF16),
            V((CONV, STATE_WIDTH), BF16),
            V((2, TOK, FEAT), BF16),
            V((2, TOK, FEAT), BF16),
            V((2, 2, TOK, STATE_WIDTH), BF16),
            V((16, 2, TOK), F32),
            V((CONV, FEAT), BF16),
            V((2, CONV, STATE_WIDTH), BF16),
            V((EDGE, FEAT), BF16),
            V((2, EDGE, STATE_WIDTH), BF16),
            V((2, TOK, HALF), BF16),
            V((2, TOK, HALF), F32),
            V((2, TOK, STATE_WIDTH), BF16),
            V((HALF, STATE_WIDTH), BF16),
            V((8, 1, 128), F32),
            V((CHIPS, 1, 128), F32),
            V((CHIPS, HEAD_WIDTH, STATE_WIDTH), BF16),
            V((CHIPS, HEAD_WIDTH, STATE_WIDTH), BF16),
            V((FEAT, STATE_WIDTH), BF16),
            V((2, TOK, FEAT), BF16),
            V((2, 2, TOK, STATE_WIDTH), BF16),
            V((2, TOK, FEAT), F32),
            V((2, TOK, FEAT), F32),
            V((2, TOK, TOK), F32),
            V((2, TOK, 128), F32),
            V((2, TOK, 128), F32),
            V((2, TOK, FEAT), BF16),
            pltpu.SemaphoreType.DMA((N_LOCAL,)),
            pltpu.SemaphoreType.DMA((N_SEND,)),
            pltpu.SemaphoreType.DMA((N_RECV,)),
        ],
        compiler_params=pltpu.CompilerParams(
            collective_id=0, has_side_effects=True, vmem_limit_bytes=60 << 20
        ),
        name="layer",
    )(
        prompt_inner,
        prompt_proj,
        prompt_step,
        completion_inner,
        completion_gate,
        completion_projections,
        sample_step,
        sample_length,
        decay_log.reshape(1, STATE_HEADS),
        conv_inner,
        conv_proj,
        norm_gain.reshape(1, FEAT),
    )


def solution(mesh):
    placed = (
        P("prompt", "comp"),
        P("prompt", None),
        P("comp", "prompt"),
        P("comp", None, "prompt"),
        P("comp", None, "prompt"),
        P("comp", None, None),
        P("prompt", "comp", None),
        P("comp"),
        P(),
        P(),
        P(),
        P("prompt"),
    )
    return jax.shard_map(
        local, mesh=mesh, in_specs=placed, out_specs=P("comp", None, "prompt"), check_vma=False
    )
```

```python
import functools

import jax
import jax.numpy as jnp
from jax import lax
from jax.experimental import pallas as pl
from jax.experimental.pallas import tpu as pltpu
from jax.sharding import PartitionSpec as P

STATE_HEADS = 256
HEAD_WIDTH = 64
STATE_WIDTH = 256
STATE_GROUPS = 8
CONV = 4
EPS = 1e-05
LOG2E = 1.4426950408889634

MESH = pl.DeviceIdType.MESH
F32 = jnp.float32
BF16 = jnp.bfloat16

ROWS = 16
COLS = 16
CHIPS = 8
TOK = 256
FEAT = 1024
HALF = 512
GROUP_HEADS = 32
PROJ_C = STATE_GROUPS * STATE_WIDTH

EDGE = 8
HALVES = 2
PIECE = HEAD_WIDTH // HALVES

R_SIB, R_HALO, R_TAIL, R_MLOG, R_LOG, R_MID = 0, 3, 5, 7, 15, 23
R_RED = R_MID + CHIPS * HALVES
R_AG = R_RED + CHIPS * HALVES
R_SQ = R_AG + COLS * HALVES
N_RECV = R_SQ + 2
S_SIB, S_HALO, S_TX, S_RELAY, S_TB = 0, 3, 7, 8, 23
S_MLOG = S_TB + 15
S_LOG = S_MLOG + 8
S_MID = S_LOG + 8
S_RED = S_MID + CHIPS * HALVES
S_AG = S_RED + CHIPS * HALVES
S_SQ = S_AG + (COLS - 1) * HALVES
N_SEND = S_SQ + 2
(L_PX, L_PB, L_PS, L_WX, L_WB, L_CX, L_CG, L_CB, L_CC, L_SS, L_WCX, L_WCB, L_WCC, L_TX, L_TB, L_TC, L_LEN, L_LOG, L_GAIN, L_OUT) = range(20)
N_LOCAL = 21


def silu(v):
    h = 0.5 * v
    return h + h * jnp.tanh(h)


def softplus(v):
    return jnp.maximum(v, 0.0) + jnp.log1p(jnp.exp(-jnp.abs(v)))


def split3(v):
    a = v.astype(BF16)
    r = v - a.astype(F32)
    b = r.astype(BF16)
    c = (r - b.astype(F32)).astype(BF16)
    return a, b, c


def dot_nt(a, b):
    return lax.dot_general(a, b, (((1,), (1,)), ((), ())), preferred_element_type=F32)


def dot_tn(a, b):
    return lax.dot_general(a, b, (((0,), (0,)), ((), ())), preferred_element_type=F32)


def convolve(x, taps):
    total = x * taps[3:4]
    for lag in (1, 2, 3):
        total = total + pltpu.roll(x, lag, 0) * taps[3 - lag : 4 - lag]
    return silu(total)


def causal_conv(src, lead, taps):
    return convolve(jnp.concatenate([lead.astype(F32), src.astype(F32)], axis=0), taps)[EDGE:]


def pick_rows(row, first, count):
    lanes = lax.broadcasted_iota(jnp.int32, (count, row.shape[1]), 1)
    heads = first + lax.broadcasted_iota(jnp.int32, (count, row.shape[1]), 0)
    wide = jnp.broadcast_to(row, (count, row.shape[1]))
    return jnp.sum(jnp.where(lanes == heads, wide, 0.0), axis=1, keepdims=True)


def kernel(
    inner, proj, pstep, cin, gate, cproj, sstep, slen_in, dlog_in, cvi, cvp, gain_in, out,
    px, pb, ps, hx, hb, wx, wb, cx, cg, cbc, ss, wcx, wcbc, tx, tbc,
    trow, tpack, xw, wide, bb, base, st, logs, midlog, redlog, mid, red, stf, xcv, bcv, part, coef, scores, sq, sqs, obuf,
    slen, dlog, gain, lsem, ssem, rsem,
):
    p = lax.axis_index("prompt")
    c = lax.axis_index("comp")
    z = p // 2
    k = p % 2
    other = 1 - k
    sib = p + 1 - 2 * k
    group_col = c // 2
    group_row = p // 2
    kk = c // 8
    c_core = c % 2
    no = jnp.logical_not
    both = jnp.logical_and

    def ds(start, size):
        return pl.ds(pl.multiple_of(start, size), size)

    def local(src, dst, sem):
        copy = pltpu.make_async_copy(src, dst, lsem.at[sem])
        copy.start()
        return copy

    def remote(src, dst, send, recv, row, col):
        return pltpu.make_async_remote_copy(
            src_ref=src, dst_ref=dst, send_sem=ssem.at[send], recv_sem=rsem.at[recv],
            device_id=(row, col), device_id_type=MESH,
        )

    def arrived(dst, recv):
        remote(dst, dst, 0, recv, p, c).wait_recv()

    barrier = pltpu.get_barrier_semaphore()

    def greet(row, col):
        pl.semaphore_signal(barrier, inc=1, device_id=(row, col), device_id_type=MESH)

    tail_self = both(p == ROWS - 1, c == COLS - 1)
    mid_self = both(kk == k, c_core == k)
    for step in (4, 3, 5, 2, 6, 1, 7):
        greet(lax.rem(p + 2 * step, ROWS), c)

    @pl.when(z > 0)
    def _():
        greet(2 * z - 1, c)

    @pl.when(both(p == c, p < ROWS - 1))
    def _():
        greet(ROWS - 1, c)

    @pl.when(p < ROWS - 1)
    def _():
        greet(ROWS - 1, c)

    for j in range(CHIPS):
        @pl.when(no(both(mid_self, c // 2 == j)))
        def _():
            greet(2 * z + kk, 2 * j + k)

    for step in range(1, COLS):
        greet(p, lax.rem(c + step, COLS))

    greet(sib, c)

    b_col = group_col * STATE_WIDTH
    b_row = group_row * STATE_WIDTH
    copies = {}
    copies[L_LOG] = local(dlog_in, dlog, L_LOG)
    copies[L_PS] = local(pstep.at[ds(8 * k, 8), :], ps.at[k], L_PS)
    copies[L_PB] = local(proj.at[:, ds(b_col, STATE_WIDTH)], pb.at[k], L_PB)
    copies[L_WB] = local(cvp.at[:, ds(b_col, STATE_WIDTH)], wb, L_WB)
    copies[L_PX] = local(inner.at[:, ds(k * HALF, HALF)], px.at[k], L_PX)
    copies[L_WX] = local(cvi.at[:, ds(c * FEAT + k * HALF, HALF)], wx, L_WX)

    last_row = (p == ROWS - 1).astype(jnp.int32)
    halo_out = both(k == 1, p < ROWS - 1)
    expected = (
        1 + 2 * halo_out.astype(jnp.int32)
        + CHIPS - mid_self.astype(jnp.int32) + CHIPS - 1 + COLS - 1
        + last_row * ROWS - tail_self.astype(jnp.int32)
    )
    pl.semaphore_wait(barrier, expected)

    edge_rows = pl.ds(TOK - EDGE, EDGE)
    sib_copies = [
        remote(pstep.at[ds(8 * other, 8), :], ps.at[k], S_SIB, R_SIB, sib, c),
        remote(proj.at[:, ds(b_col, STATE_WIDTH)], pb.at[k], S_SIB + 1, R_SIB + 1, sib, c),
        remote(inner.at[:, ds(other * HALF, HALF)], px.at[k], S_SIB + 2, R_SIB + 2, sib, c),
    ]

    def halo_copies():
        found = []
        for core in range(2):
            found.append(
                remote(
                    inner.at[edge_rows, pl.ds(core * HALF, HALF)], hx,
                    S_HALO + 2 * core, R_HALO, p + 1 + core, c,
                )
            )
            found.append(
                remote(
                    proj.at[edge_rows, ds(b_col, STATE_WIDTH)], hb,
                    S_HALO + 2 * core + 1, R_HALO + 1, p + 1 + core, c,
                )
            )
        return found

    @pl.when(halo_out)
    def _():
        for copy in halo_copies():
            copy.start()

    for copy in sib_copies:
        copy.start()

    @pl.when(z == 0)
    def _():
        hx[...] = jnp.zeros_like(hx)
        hb[...] = jnp.zeros_like(hb)

    def tail_copy():
        return remote(inner.at[edge_rows, :], tx, S_TX, R_TAIL, c, c)

    def relay_copy(step):
        return remote(tx, tx, S_RELAY + step - 1, R_TAIL, p, lax.rem(c + step, COLS))

    def tail_bc(j):
        return remote(tpack.at[j // 2], tbc, S_TB + j, R_TAIL + 1, j, c)

    def tail_local():
        return pltpu.make_async_copy(inner.at[edge_rows, :], tx, lsem.at[L_TX])

    def tail_proj():
        return pltpu.make_async_copy(proj.at[edge_rows, :], trow, lsem.at[L_TB])

    tail_out = both(p == ROWS - 1, c < COLS - 1)

    @pl.when(tail_out)
    def _():
        tail_copy().start()

    @pl.when(tail_self)
    def _():
        tail_local().start()

    @pl.when(p == ROWS - 1)
    def _():
        tail_proj().start()

    copies[L_SS] = local(sstep, ss, L_SS)
    copies[L_CX] = local(cin, cx, L_CX)
    copies[L_WCX] = local(cvi.at[:, ds(p * FEAT, FEAT)], wcx, L_WCX)
    copies[L_CB] = local(cproj.at[:, :, ds(b_row, STATE_WIDTH)], cbc.at[0], L_CB)
    copies[L_CC] = local(cproj.at[:, :, ds(PROJ_C + b_row, STATE_WIDTH)], cbc.at[1], L_CC)
    copies[L_WCB] = local(cvp.at[:, ds(b_row, STATE_WIDTH)], wcbc.at[0], L_WCB)
    copies[L_WCC] = local(cvp.at[:, ds(PROJ_C + b_row, STATE_WIDTH)], wcbc.at[1], L_WCC)
    copies[L_CG] = local(gate, cg, L_CG)
    copies[L_GAIN] = local(gain_in, gain, L_GAIN)
    copies[L_LEN] = local(slen_in, slen, L_LEN)

    row_id = lax.broadcasted_iota(jnp.int32, (TOK, TOK), 0)
    col_id = lax.broadcasted_iota(jnp.int32, (TOK, TOK), 1)
    tri = jnp.where(col_id <= row_id, 1.0, 0.0).astype(BF16)

    def running(values):
        a, b, d = split3(values)
        return dot_nt(a, tri) + (dot_nt(b, tri) + dot_nt(d, tri))

    def running_t(values):
        a, b, d = split3(values)
        return dot_nt(tri, a) + (dot_nt(tri, b) + dot_nt(tri, d))

    copies[L_LOG].wait()
    rate_col = jnp.exp(pick_rows(dlog[...], c * 16 + 8 * k, 8)) * LOG2E
    spread = jnp.where(
        lax.broadcasted_iota(jnp.int32, (24, HALF), 1) // HEAD_WIDTH
        == lax.broadcasted_iota(jnp.int32, (24, HALF), 0) % 8,
        1.0,
        0.0,
    ).astype(BF16)

    def weigh(block):
        dt = softplus(ps[block])
        run = running(-rate_col * dt)
        total = run[:, TOK - 1 :]
        weight = jnp.exp2(total - run) * dt
        pieces = jnp.concatenate([piece.astype(F32) for piece in split3(weight)], axis=0).astype(BF16)
        wide[block] = dot_tn(pieces, spread)
        return total

    def conv_b(block):
        x = pb[block].astype(F32)
        bb[block] = convolve(x, wb[...].astype(F32)).astype(BF16)

    def conv_x(block):
        for quarter in range(4):
            cols = pl.ds(quarter * 128, 128)
            x = px[block, :, cols].astype(F32)
            xw[block, :, cols] = (convolve(x, wx[:, cols].astype(F32)) * wide[block, :, cols]).astype(BF16)

    copies[L_PS].wait()
    total_own = weigh(k)
    copies[L_PB].wait()
    copies[L_WB].wait()
    conv_b(k)
    copies[L_PX].wait()
    copies[L_WX].wait()
    conv_x(k)

    @pl.when(p == ROWS - 1)
    def _():
        tail_proj().wait()
        for group in range(STATE_GROUPS):
            for which in range(2):
                first = which * PROJ_C + group * STATE_WIDTH
                tpack[group, which] = trow[:, first : first + STATE_WIDTH]
        tbc[...] = tpack[group_row]
        for j in range(ROWS - 1):
            tail_bc(j).start()

    arrived(ps.at[other], R_SIB)
    total_sib = weigh(other)
    total1 = jnp.where(k == 1, total_own, total_sib)
    total_chip = jnp.broadcast_to(total_own + total_sib, (8, 128))
    for i in range(8):
        logs[i] = total_chip[i : i + 1]

    def mid_own(i):
        return both(mid_self, 8 * k + i == c)

    def mlog_copy(i):
        return remote(
            logs.at[i], midlog.at[c // 2], S_MLOG + i, R_MLOG + c // 2, 2 * z + c_core, 8 * k + i
        )

    for i in range(8):
        @pl.when(no(mid_own(i)))
        def _():
            mlog_copy(i).start()

        @pl.when(mid_own(i))
        def _():
            midlog[c // 2] = logs[i]

    arrived(pb.at[other], R_SIB + 1)
    arrived(px.at[other], R_SIB + 2)
    conv_b(other)
    conv_x(other)

    taps_b = wb[...].astype(F32)
    taps_x = wx[...].astype(F32)
    bb[1, :16, :] = causal_conv(pb[1, :16, :], pb[0, edge_rows, :], taps_b).astype(BF16)
    xw[1, :16, :] = (causal_conv(px[1, :16, :], px[0, edge_rows, :], taps_x) * wide[1, :16, :]).astype(BF16)
    xw[0, :16, :] = jnp.zeros((16, HALF), BF16)
    decay1 = jnp.exp2(jnp.broadcast_to(total1, (8, STATE_WIDTH)))
    for pair in range(4):
        cols = pl.ds(pair * 128, 128)
        first = dot_tn(xw[0, :, cols], bb[0])
        second = dot_tn(xw[1, :, cols], bb[1])
        for side in range(2):
            i = 2 * pair + side
            rows = slice(side * HEAD_WIDTH, (side + 1) * HEAD_WIDTH)
            base[pl.ds(i * HEAD_WIDTH, HEAD_WIDTH), :] = first[rows] * decay1[i : i + 1] + second[rows]

    @pl.when(z > 0)
    def _():
        arrived(hx, R_HALO)
        arrived(hb, R_HALO + 1)

    edge_b = causal_conv(pb[0, :16, :], hb[...], taps_b).astype(BF16)
    edge_x = (causal_conv(px[0, :16, :], hx[...], taps_x) * wide[0, :16, :]).astype(BF16)

    def mid_copy(i, half):
        rows = pl.ds(i * HEAD_WIDTH + half * PIECE, PIECE)
        return remote(
            st.at[rows, :], mid.at[c // 2, pl.ds(half * PIECE, PIECE), :],
            S_MID + 2 * i + half, R_MID + 2 * (c // 2) + half, 2 * z + c_core, 8 * k + i,
        )

    for pair in range(4):
        edge = dot_tn(edge_x[:, pair * 128 : pair * 128 + 128], edge_b)
        for side in range(2):
            i = 2 * pair + side
            rows = slice(side * HEAD_WIDTH, (side + 1) * HEAD_WIDTH)
            mine_i = pl.ds(i * HEAD_WIDTH, HEAD_WIDTH)
            st[mine_i, :] = (base[mine_i, :] + edge[rows] * decay1[i : i + 1]).astype(BF16)

            @pl.when(no(mid_own(i)))
            def _():
                for half in range(HALVES):
                    mid_copy(i, half).start()

            @pl.when(mid_own(i))
            def _():
                mid[c // 2] = st[pl.ds(i * HEAD_WIDTH, HEAD_WIDTH), :]

    @pl.when(both(p == c, no(tail_self)))
    def _():
        arrived(tx, R_TAIL)

    @pl.when(tail_self)
    def _():
        tail_local().wait()

    @pl.when(p == c)
    def _():
        for step in range(1, COLS):
            relay_copy(step).start()

    copies[L_CB].wait()
    copies[L_CC].wait()
    copies[L_WCB].wait()
    copies[L_WCC].wait()
    copies[L_WCX].wait()
    copies[L_CX].wait()
    copies[L_CG].wait()
    for slot in range(2):
        for eighth in range(8):
            cols = pl.ds(eighth * 128, 128)
            x = cx[slot, :, cols].astype(F32)
            xcv[slot, :, cols] = convolve(x, wcx[:, cols].astype(F32)).astype(BF16)
        for which in range(2):
            x = cbc[which, slot].astype(F32)
            bcv[which, slot] = convolve(x, wcbc[which].astype(F32)).astype(BF16)

    copies[L_SS].wait()
    rate_row = jnp.exp(pick_rows(dlog[...], p * 16, 16)) * LOG2E
    log_step = []
    raw = []
    for slot in range(2):
        dt = softplus(ss[:, slot, :])
        raw.append(-rate_row * dt)
        log_step.append(jnp.log2(dt))
    raw = jnp.concatenate(raw, axis=0)
    cum = running(raw)
    cum_t = running_t(raw)
    shifted = cum - jnp.concatenate(log_step, axis=0)

    def red_copy(j, half):
        rows = pl.ds(half * PIECE, PIECE)
        return remote(
            mid.at[j, rows, :], red.at[z, rows, :],
            S_RED + 2 * j + half, R_RED + 2 * z + half, 2 * j + k, c,
        )

    def log_copy(j):
        return remote(midlog.at[j], redlog.at[z], S_LOG + j, R_LOG + z, 2 * j + k, c)

    for j in range(CHIPS):
        @pl.when(no(both(mid_self, c // 2 == j)))
        def _():
            arrived(midlog.at[j], R_MLOG + j)

        @pl.when(z != j)
        def _():
            log_copy(j).start()

        @pl.when(z == j)
        def _():
            redlog[z] = midlog[j]

    for half in range(HALVES):
        rows = pl.ds(half * PIECE, PIECE)
        for j in range(CHIPS):
            @pl.when(no(both(mid_self, c // 2 == j)))
            def _():
                arrived(mid.at[j, rows, :], R_MID + 2 * j + half)

            @pl.when(z != j)
            def _():
                red_copy(j, half).start()

            @pl.when(z == j)
            def _():
                red[z, rows, :] = mid[j, rows, :]

    @pl.when(p != c)
    def _():
        arrived(tx, R_TAIL)

    @pl.when(p < ROWS - 1)
    def _():
        arrived(tbc, R_TAIL + 1)

    for slot in range(2):
        xcv[slot, :16, :] = causal_conv(cx[slot, :16, :], tx[...], wcx[...].astype(F32)).astype(BF16)
        for which in range(2):
            bcv[which, slot, :16, :] = causal_conv(
                cbc[which, slot, :16, :], tbc[which], wcbc[which].astype(F32)
            ).astype(BF16)
        scores[slot] = dot_nt(bcv[1, slot], bcv[0, slot])

    lane_low = lax.broadcasted_iota(jnp.int32, (TOK, 128), 1) < HEAD_WIDTH
    causal = (
        lax.broadcasted_iota(jnp.int32, (128, 128), 1) <= lax.broadcasted_iota(jnp.int32, (128, 128), 0)
    )

    def intra(slot, pair):
        cols = pl.ds(pair * 128, 128)
        x = xcv[slot, :, cols]
        made = []
        spread_logs = []
        for h in (2 * pair, 2 * pair + 1):
            at = slot * 16 + h
            down = jnp.broadcast_to(cum_t[:, at : at + 1], (TOK, 128))
            left = down - shifted[at : at + 1, :128]
            right = down[128:] - shifted[at : at + 1, 128:]
            top = jnp.exp2(jnp.where(causal, left[:128], -jnp.inf)) * scores[slot, :128, :128]
            low = jnp.exp2(left[128:]) * scores[slot, 128:, :128]
            diag = jnp.exp2(jnp.where(causal, right, -jnp.inf)) * scores[slot, 128:, 128:]
            y0 = jnp.dot(top.astype(BF16), x[:128], preferred_element_type=F32)
            y1 = jnp.dot(low.astype(BF16), x[:128], preferred_element_type=F32) + jnp.dot(
                diag.astype(BF16), x[128:], preferred_element_type=F32
            )
            made.append(jnp.concatenate([y0, y1], axis=0))
            spread_logs.append(down)
        g = silu(cg[slot, :, cols].astype(F32))
        part[slot, :, cols] = jnp.where(lane_low, made[0], made[1]) * g
        coef[slot, :, cols] = jnp.exp2(jnp.where(lane_low, spread_logs[0], spread_logs[1])) * g

    for slot in range(2):
        for pair in range(8):
            intra(slot, pair)

    for chip in range(CHIPS):
        @pl.when(z != chip)
        def _():
            arrived(redlog.at[chip], R_LOG + chip)

    later = jnp.zeros((1, 128), F32)
    scales = []
    for chip in range(CHIPS - 1, -1, -1):
        scales.insert(0, jnp.exp2(later)[:, :1])
        later = later + redlog[chip]

    def mine(half):
        return ds(c * HEAD_WIDTH + half * PIECE, PIECE)

    def ag_copy(step, half):
        return remote(
            stf.at[mine(half), :], stf.at[mine(half), :],
            S_AG + HALVES * (step - 1) + half, R_AG + HALVES * c + half, p, lax.rem(c + step, COLS),
        )

    for half in range(HALVES):
        rows = pl.ds(half * PIECE, PIECE)
        for chip in range(CHIPS):
            @pl.when(z != chip)
            def _():
                arrived(red.at[chip, rows, :], R_RED + 2 * chip + half)

        state = None
        for chip in range(CHIPS):
            term = red[chip, rows, :].astype(F32) * scales[chip]
            state = term if state is None else state + term
        stf[mine(half), :] = state.astype(BF16)
        for step in range(1, COLS):
            ag_copy(step, half).start()

    def sq_copy(slot):
        return remote(sq.at[slot], sqs.at[slot], S_SQ + slot, R_SQ + slot, sib, c)

    for chunk in range(4):
        for source in range(4 * chunk, 4 * chunk + 4):
            @pl.when(c != source)
            def _():
                for half in range(HALVES):
                    arrived(
                        stf.at[pl.ds(source * HEAD_WIDTH + half * PIECE, PIECE), :],
                        R_AG + HALVES * source + half,
                    )

        cols = pl.ds(chunk * 256, 256)
        for slot in range(2):
            read = dot_nt(bcv[1, slot], stf[cols, :])
            gated = part[slot, :, cols] + coef[slot, :, cols] * read
            part[slot, :, cols] = gated
            squares = gated[:, :128] * gated[:, :128] + gated[:, 128:] * gated[:, 128:]
            sq[slot] = squares if chunk == 0 else sq[slot] + squares
            if chunk == 3:
                sq_copy(slot).start()

    copies[L_GAIN].wait()
    copies[L_LEN].wait()
    gains = gain[...]
    position = lax.broadcasted_iota(jnp.int32, (TOK, 1), 0)
    outs = []
    for slot in range(2):
        arrived(sqs.at[slot], R_SQ + slot)
        mean = jnp.sum(sq[slot] + sqs[slot], axis=1, keepdims=True) * (1.0 / (GROUP_HEADS * HEAD_WIDTH))
        scale = jnp.where(position < slen[slot], lax.rsqrt(mean + EPS), 0.0)
        obuf[slot] = (part[slot] * scale * gains).astype(BF16)
        copy = pltpu.make_async_copy(obuf.at[slot], out.at[slot], lsem.at[L_OUT + slot])
        copy.start()
        outs.append(copy)

    for copy in sib_copies:
        copy.wait_send()

    @pl.when(halo_out)
    def _():
        for copy in halo_copies():
            copy.wait_send()

    @pl.when(tail_out)
    def _():
        tail_copy().wait_send()

    @pl.when(p == c)
    def _():
        for step in range(1, COLS):
            relay_copy(step).wait_send()

    @pl.when(p == ROWS - 1)
    def _():
        for j in range(ROWS - 1):
            tail_bc(j).wait_send()

    for i in range(8):
        @pl.when(no(mid_own(i)))
        def _():
            mlog_copy(i).wait_send()
            for half in range(HALVES):
                mid_copy(i, half).wait_send()

    for half in range(HALVES):
        for j in range(CHIPS):
            @pl.when(z != j)
            def _():
                red_copy(j, half).wait_send()
                if half == 0:
                    log_copy(j).wait_send()

        for step in range(1, COLS):
            ag_copy(step, half).wait_send()
    for slot in range(2):
        sq_copy(slot).wait_send()
    for copy in outs:
        copy.wait()


def local(
    prompt_inner,
    prompt_proj,
    prompt_step,
    completion_inner,
    completion_gate,
    completion_projections,
    sample_step,
    sample_length,
    decay_log,
    conv_inner,
    conv_proj,
    norm_gain,
):
    hbm = pl.BlockSpec(memory_space=pl.ANY)
    V = pltpu.VMEM
    layer = pl.pallas_call(
        kernel,
        out_shape=jax.ShapeDtypeStruct(completion_inner.shape, BF16),
        in_specs=[hbm] * 12,
        out_specs=hbm,
        scratch_shapes=[
            V((2, TOK, HALF), BF16),
            V((2, TOK, STATE_WIDTH), BF16),
            V((2, 8, TOK), F32),
            V((EDGE, HALF), BF16),
            V((EDGE, STATE_WIDTH), BF16),
            V((CONV, HALF), BF16),
            V((CONV, STATE_WIDTH), BF16),
            V((2, TOK, FEAT), BF16),
            V((2, TOK, FEAT), BF16),
            V((2, 2, TOK, STATE_WIDTH), BF16),
            V((16, 2, TOK), F32),
            V((CONV, FEAT), BF16),
            V((2, CONV, STATE_WIDTH), BF16),
            V((EDGE, FEAT), BF16),
            V((2, EDGE, STATE_WIDTH), BF16),
            V((EDGE, 2 * PROJ_C), BF16),
            V((STATE_GROUPS, 2, EDGE, STATE_WIDTH), BF16),
            V((2, TOK, HALF), BF16),
            V((2, TOK, HALF), F32),
            V((2, TOK, STATE_WIDTH), BF16),
            V((HALF, STATE_WIDTH), F32),
            V((HALF, STATE_WIDTH), BF16),
            V((8, 1, 128), F32),
            V((CHIPS, 1, 128), F32),
            V((CHIPS, 1, 128), F32),
            V((CHIPS, HEAD_WIDTH, STATE_WIDTH), BF16),
            V((CHIPS, HEAD_WIDTH, STATE_WIDTH), BF16),
            V((FEAT, STATE_WIDTH), BF16),
            V((2, TOK, FEAT), BF16),
            V((2, 2, TOK, STATE_WIDTH), BF16),
            V((2, TOK, FEAT), F32),
            V((2, TOK, FEAT), F32),
            V((2, TOK, TOK), F32),
            V((2, TOK, 128), F32),
            V((2, TOK, 128), F32),
            V((2, TOK, FEAT), BF16),
            pltpu.SMEM((2,), jnp.int32),
            V((1, STATE_HEADS), F32),
            V((1, FEAT), F32),
            pltpu.SemaphoreType.DMA((N_LOCAL,)),
            pltpu.SemaphoreType.DMA((N_SEND,)),
            pltpu.SemaphoreType.DMA((N_RECV,)),
        ],
        compiler_params=pltpu.CompilerParams(
            collective_id=0, has_side_effects=True, vmem_limit_bytes=48 << 20
        ),
        name="layer",
    )
    arrays = (
        prompt_inner,
        prompt_proj,
        prompt_step,
        completion_inner,
        completion_gate,
        completion_projections,
        sample_step,
        sample_length,
        decay_log.reshape(1, STATE_HEADS),
        conv_inner,
        conv_proj,
        norm_gain.reshape(1, FEAT),
    )
    return layer(*[pltpu.with_memory_space_constraint(array, pltpu.HBM) for array in arrays])


def solution(mesh):
    placed = (
        P("prompt", "comp"),
        P("prompt", None),
        P("comp", "prompt"),
        P("comp", None, "prompt"),
        P("comp", None, "prompt"),
        P("comp", None, None),
        P("prompt", "comp", None),
        P("comp"),
        P(),
        P(),
        P(),
        P("prompt"),
    )
    return jax.shard_map(
        local, mesh=mesh, in_specs=placed, out_specs=P("comp", None, "prompt"), check_vma=False
    )
```

```python
import functools

import jax
import jax.numpy as jnp
from jax import lax
from jax.experimental import pallas as pl
from jax.experimental.pallas import tpu as pltpu
from jax.sharding import PartitionSpec as P

STATE_HEADS = 256
HEAD_WIDTH = 64
STATE_WIDTH = 256
STATE_GROUPS = 8
CONV = 4
EPS = 1e-05
LOG2E = 1.4426950408889634

MESH = pl.DeviceIdType.MESH
F32 = jnp.float32
BF16 = jnp.bfloat16

ROWS = 16
COLS = 16
CHIPS = 8
TOK = 256
FEAT = 1024
HALF = 512
GROUP_HEADS = 32
PROJ_C = STATE_GROUPS * STATE_WIDTH

EDGE = 8
HALVES = 2
PIECE = HEAD_WIDTH // HALVES

R_SIB, R_HALO, R_TAIL, R_MLOG, R_LOG, R_MID = 0, 3, 5, 7, 15, 23
R_RED = R_MID + CHIPS * HALVES
R_AG = R_RED + CHIPS * HALVES
R_SQ = R_AG + COLS * HALVES
N_RECV = R_SQ + 2
S_SIB, S_HALO, S_TX, S_RELAY, S_TB = 0, 3, 7, 8, 23
S_MLOG = S_TB + 15
S_LOG = S_MLOG + 8
S_MID = S_LOG + 8
S_RED = S_MID + CHIPS * HALVES
S_AG = S_RED + CHIPS * HALVES
S_SQ = S_AG + (COLS - 1) * HALVES
N_SEND = S_SQ + 2
(L_PX, L_PB, L_PS, L_WX, L_WB, L_CX, L_CG, L_CB, L_CC, L_SS, L_WCX, L_WCB, L_WCC, L_TX, L_TB, L_TC, L_LEN, L_LOG, L_GAIN, L_OUT) = range(20)
N_LOCAL = 21


def silu(v):
    h = 0.5 * v
    return h + h * jnp.tanh(h)


def softplus(v):
    return jnp.maximum(v, 0.0) + jnp.log1p(jnp.exp(-jnp.abs(v)))


def split3(v):
    a = v.astype(BF16)
    r = v - a.astype(F32)
    b = r.astype(BF16)
    c = (r - b.astype(F32)).astype(BF16)
    return a, b, c


def dot_nt(a, b):
    return lax.dot_general(a, b, (((1,), (1,)), ((), ())), preferred_element_type=F32)


def dot_tn(a, b):
    return lax.dot_general(a, b, (((0,), (0,)), ((), ())), preferred_element_type=F32)


def convolve(x, taps):
    total = x * taps[3:4]
    for lag in (1, 2, 3):
        total = total + pltpu.roll(x, lag, 0) * taps[3 - lag : 4 - lag]
    return silu(total)


def causal_conv(src, lead, taps):
    return convolve(jnp.concatenate([lead.astype(F32), src.astype(F32)], axis=0), taps)[EDGE:]


def pick_rows(row, first, count):
    lanes = lax.broadcasted_iota(jnp.int32, (count, row.shape[1]), 1)
    heads = first + lax.broadcasted_iota(jnp.int32, (count, row.shape[1]), 0)
    wide = jnp.broadcast_to(row, (count, row.shape[1]))
    return jnp.sum(jnp.where(lanes == heads, wide, 0.0), axis=1, keepdims=True)


def kernel(
    inner, proj, pstep, cin, gate, cproj, sstep, slen_in, dlog_in, cvi, cvp, gain_in, out,
    px, pb, ps, hx, hb, wx, wb, cx, cg, cbc, ss, wcx, wcbc, tx, tbc,
    trow, tpack, xw, wide, bb, base, st, logs, midlog, redlog, mid, red, stf, xcv, bcv, part, coef, scores, sq, sqs, obuf,
    slen, dlog, gain, lsem, ssem, rsem,
):
    p = lax.axis_index("prompt")
    c = lax.axis_index("comp")
    z = p // 2
    k = p % 2
    other = 1 - k
    sib = p + 1 - 2 * k
    group_col = c // 2
    group_row = p // 2
    kk = c // 8
    c_core = c % 2
    no = jnp.logical_not
    both = jnp.logical_and

    def ds(start, size):
        return pl.ds(pl.multiple_of(start, size), size)

    def local(src, dst, sem):
        copy = pltpu.make_async_copy(src, dst, lsem.at[sem])
        copy.start()
        return copy

    def remote(src, dst, send, recv, row, col):
        return pltpu.make_async_remote_copy(
            src_ref=src, dst_ref=dst, send_sem=ssem.at[send], recv_sem=rsem.at[recv],
            device_id=(row, col), device_id_type=MESH,
        )

    def arrived(dst, recv):
        remote(dst, dst, 0, recv, p, c).wait_recv()

    barrier = pltpu.get_barrier_semaphore()

    def greet(row, col):
        pl.semaphore_signal(barrier, inc=1, device_id=(row, col), device_id_type=MESH)

    tail_self = both(p == ROWS - 1, c == COLS - 1)
    mid_self = both(kk == k, c_core == k)
    for step in (4, 3, 5, 2, 6, 1, 7):
        greet(lax.rem(p + 2 * step, ROWS), c)

    @pl.when(z > 0)
    def _():
        greet(2 * z - 1, c)

    @pl.when(both(p == c, p < ROWS - 1))
    def _():
        greet(ROWS - 1, c)

    @pl.when(p < ROWS - 1)
    def _():
        greet(ROWS - 1, c)

    for j in range(CHIPS):
        @pl.when(no(both(mid_self, c // 2 == j)))
        def _():
            greet(2 * z + kk, 2 * j + k)

    for step in range(1, COLS):
        greet(p, lax.rem(c + step, COLS))

    greet(sib, c)

    b_col = group_col * STATE_WIDTH
    b_row = group_row * STATE_WIDTH
    copies = {}
    copies[L_LOG] = local(dlog_in, dlog, L_LOG)
    copies[L_PS] = local(pstep.at[ds(8 * k, 8), :], ps.at[k], L_PS)
    copies[L_PB] = local(proj.at[:, ds(b_col, STATE_WIDTH)], pb.at[k], L_PB)
    copies[L_WB] = local(cvp.at[:, ds(b_col, STATE_WIDTH)], wb, L_WB)
    copies[L_PX] = local(inner.at[:, ds(k * HALF, HALF)], px.at[k], L_PX)
    copies[L_WX] = local(cvi.at[:, ds(c * FEAT + k * HALF, HALF)], wx, L_WX)

    last_row = (p == ROWS - 1).astype(jnp.int32)
    halo_out = both(k == 1, p < ROWS - 1)
    expected = (
        1 + 2 * halo_out.astype(jnp.int32)
        + CHIPS - mid_self.astype(jnp.int32) + CHIPS - 1 + COLS - 1
        + last_row * ROWS - tail_self.astype(jnp.int32)
    )
    pl.semaphore_wait(barrier, expected)

    edge_rows = pl.ds(TOK - EDGE, EDGE)
    sib_copies = [
        remote(pstep.at[ds(8 * other, 8), :], ps.at[k], S_SIB, R_SIB, sib, c),
        remote(proj.at[:, ds(b_col, STATE_WIDTH)], pb.at[k], S_SIB + 1, R_SIB + 1, sib, c),
        remote(inner.at[:, ds(other * HALF, HALF)], px.at[k], S_SIB + 2, R_SIB + 2, sib, c),
    ]

    def halo_copies():
        found = []
        for core in range(2):
            found.append(
                remote(
                    inner.at[edge_rows, pl.ds(core * HALF, HALF)], hx,
                    S_HALO + 2 * core, R_HALO, p + 1 + core, c,
                )
            )
            found.append(
                remote(
                    proj.at[edge_rows, ds(b_col, STATE_WIDTH)], hb,
                    S_HALO + 2 * core + 1, R_HALO + 1, p + 1 + core, c,
                )
            )
        return found

    @pl.when(halo_out)
    def _():
        for copy in halo_copies():
            copy.start()

    for copy in sib_copies:
        copy.start()

    @pl.when(z == 0)
    def _():
        hx[...] = jnp.zeros_like(hx)
        hb[...] = jnp.zeros_like(hb)

    def tail_copy():
        return remote(inner.at[edge_rows, :], tx, S_TX, R_TAIL, c, c)

    def relay_copy(step):
        return remote(tx, tx, S_RELAY + step - 1, R_TAIL, p, lax.rem(c + step, COLS))

    def tail_bc(j):
        return remote(tpack.at[j // 2], tbc, S_TB + j, R_TAIL + 1, j, c)

    def tail_local():
        return pltpu.make_async_copy(inner.at[edge_rows, :], tx, lsem.at[L_TX])

    def tail_proj():
        return pltpu.make_async_copy(proj.at[edge_rows, :], trow, lsem.at[L_TB])

    tail_out = both(p == ROWS - 1, c < COLS - 1)

    @pl.when(tail_out)
    def _():
        tail_copy().start()

    @pl.when(tail_self)
    def _():
        tail_local().start()

    @pl.when(p == ROWS - 1)
    def _():
        tail_proj().start()

    copies[L_SS] = local(sstep, ss, L_SS)
    copies[L_CX] = local(cin, cx, L_CX)
    copies[L_WCX] = local(cvi.at[:, ds(p * FEAT, FEAT)], wcx, L_WCX)
    copies[L_CB] = local(cproj.at[:, :, ds(b_row, STATE_WIDTH)], cbc.at[0], L_CB)
    copies[L_CC] = local(cproj.at[:, :, ds(PROJ_C + b_row, STATE_WIDTH)], cbc.at[1], L_CC)
    copies[L_WCB] = local(cvp.at[:, ds(b_row, STATE_WIDTH)], wcbc.at[0], L_WCB)
    copies[L_WCC] = local(cvp.at[:, ds(PROJ_C + b_row, STATE_WIDTH)], wcbc.at[1], L_WCC)
    copies[L_CG] = local(gate, cg, L_CG)
    copies[L_GAIN] = local(gain_in, gain, L_GAIN)
    copies[L_LEN] = local(slen_in, slen, L_LEN)

    row_id = lax.broadcasted_iota(jnp.int32, (TOK, TOK), 0)
    col_id = lax.broadcasted_iota(jnp.int32, (TOK, TOK), 1)
    tri = jnp.where(col_id <= row_id, 1.0, 0.0).astype(BF16)

    def running(values):
        a, b, d = split3(values)
        return dot_nt(a, tri) + (dot_nt(b, tri) + dot_nt(d, tri))

    def running_t(values):
        a, b, d = split3(values)
        return dot_nt(tri, a) + (dot_nt(tri, b) + dot_nt(tri, d))

    copies[L_LOG].wait()
    rate_col = jnp.exp(pick_rows(dlog[...], c * 16 + 8 * k, 8)) * LOG2E
    spread = jnp.where(
        lax.broadcasted_iota(jnp.int32, (24, HALF), 1) // HEAD_WIDTH
        == lax.broadcasted_iota(jnp.int32, (24, HALF), 0) % 8,
        1.0,
        0.0,
    ).astype(BF16)

    def weigh(block):
        dt = softplus(ps[block])
        run = running(-rate_col * dt)
        total = run[:, TOK - 1 :]
        weight = jnp.exp2(total - run) * dt
        pieces = jnp.concatenate([piece.astype(F32) for piece in split3(weight)], axis=0).astype(BF16)
        wide[block] = dot_tn(pieces, spread)
        return total

    def conv_b(block):
        x = pb[block].astype(F32)
        bb[block] = convolve(x, wb[...].astype(F32)).astype(BF16)

    def conv_x(block):
        for quarter in range(4):
            cols = pl.ds(quarter * 128, 128)
            x = px[block, :, cols].astype(F32)
            xw[block, :, cols] = (convolve(x, wx[:, cols].astype(F32)) * wide[block, :, cols]).astype(BF16)

    copies[L_PS].wait()
    total_own = weigh(k)
    copies[L_PB].wait()
    copies[L_WB].wait()
    conv_b(k)
    copies[L_PX].wait()
    copies[L_WX].wait()
    conv_x(k)

    @pl.when(p == ROWS - 1)
    def _():
        tail_proj().wait()
        for group in range(STATE_GROUPS):
            for which in range(2):
                first = which * PROJ_C + group * STATE_WIDTH
                tpack[group, which] = trow[:, first : first + STATE_WIDTH]
        tbc[...] = tpack[group_row]
        for j in range(ROWS - 1):
            tail_bc(j).start()

    arrived(ps.at[other], R_SIB)
    total_sib = weigh(other)
    total1 = jnp.where(k == 1, total_own, total_sib)
    total_chip = jnp.broadcast_to(total_own + total_sib, (8, 128))
    for i in range(8):
        logs[i] = total_chip[i : i + 1]

    def mid_own(i):
        return both(mid_self, 8 * k + i == c)

    def mlog_copy(i):
        return remote(
            logs.at[i], midlog.at[c // 2], S_MLOG + i, R_MLOG + c // 2, 2 * z + c_core, 8 * k + i
        )

    for i in range(8):
        @pl.when(no(mid_own(i)))
        def _():
            mlog_copy(i).start()

        @pl.when(mid_own(i))
        def _():
            midlog[c // 2] = logs[i]

    arrived(pb.at[other], R_SIB + 1)
    arrived(px.at[other], R_SIB + 2)
    conv_b(other)
    conv_x(other)

    taps_b = wb[...].astype(F32)
    taps_x = wx[...].astype(F32)
    bb[1, :16, :] = causal_conv(pb[1, :16, :], pb[0, edge_rows, :], taps_b).astype(BF16)
    xw[1, :16, :] = (causal_conv(px[1, :16, :], px[0, edge_rows, :], taps_x) * wide[1, :16, :]).astype(BF16)
    xw[0, :16, :] = jnp.zeros((16, HALF), BF16)
    decay1 = jnp.exp2(jnp.broadcast_to(total1, (8, STATE_WIDTH)))
    for pair in range(4):
        cols = pl.ds(pair * 128, 128)
        first = dot_tn(xw[0, :, cols], bb[0])
        second = dot_tn(xw[1, :, cols], bb[1])
        for side in range(2):
            i = 2 * pair + side
            rows = slice(side * HEAD_WIDTH, (side + 1) * HEAD_WIDTH)
            base[pl.ds(i * HEAD_WIDTH, HEAD_WIDTH), :] = first[rows] * decay1[i : i + 1] + second[rows]

    @pl.when(z > 0)
    def _():
        arrived(hx, R_HALO)
        arrived(hb, R_HALO + 1)

    edge_b = causal_conv(pb[0, :16, :], hb[...], taps_b).astype(BF16)
    edge_x = (causal_conv(px[0, :16, :], hx[...], taps_x) * wide[0, :16, :]).astype(BF16)

    def mid_copy(i, half):
        rows = pl.ds(i * HEAD_WIDTH + half * PIECE, PIECE)
        return remote(
            st.at[rows, :], mid.at[c // 2, pl.ds(half * PIECE, PIECE), :],
            S_MID + 2 * i + half, R_MID + 2 * (c // 2) + half, 2 * z + c_core, 8 * k + i,
        )

    for pair in range(4):
        edge = dot_tn(edge_x[:, pair * 128 : pair * 128 + 128], edge_b)
        for side in range(2):
            i = 2 * pair + side
            rows = slice(side * HEAD_WIDTH, (side + 1) * HEAD_WIDTH)
            mine_i = pl.ds(i * HEAD_WIDTH, HEAD_WIDTH)
            st[mine_i, :] = (base[mine_i, :] + edge[rows] * decay1[i : i + 1]).astype(BF16)

            @pl.when(no(mid_own(i)))
            def _():
                mid_copy(i, 0).start()

            @pl.when(mid_own(i))
            def _():
                mid[c // 2] = st[pl.ds(i * HEAD_WIDTH, HEAD_WIDTH), :]

    for half in range(1, HALVES):
        for i in range(8):
            @pl.when(no(mid_own(i)))
            def _():
                mid_copy(i, half).start()

    @pl.when(both(p == c, no(tail_self)))
    def _():
        arrived(tx, R_TAIL)

    @pl.when(tail_self)
    def _():
        tail_local().wait()

    @pl.when(p == c)
    def _():
        for step in range(1, COLS):
            relay_copy(step).start()

    copies[L_CB].wait()
    copies[L_CC].wait()
    copies[L_WCB].wait()
    copies[L_WCC].wait()
    copies[L_WCX].wait()
    copies[L_CX].wait()
    copies[L_CG].wait()
    for slot in range(2):
        for eighth in range(8):
            cols = pl.ds(eighth * 128, 128)
            x = cx[slot, :, cols].astype(F32)
            xcv[slot, :, cols] = convolve(x, wcx[:, cols].astype(F32)).astype(BF16)
        for which in range(2):
            x = cbc[which, slot].astype(F32)
            bcv[which, slot] = convolve(x, wcbc[which].astype(F32)).astype(BF16)

    copies[L_SS].wait()
    rate_row = jnp.exp(pick_rows(dlog[...], p * 16, 16)) * LOG2E
    log_step = []
    raw = []
    for slot in range(2):
        dt = softplus(ss[:, slot, :])
        raw.append(-rate_row * dt)
        log_step.append(jnp.log2(dt))
    raw = jnp.concatenate(raw, axis=0)
    cum = running(raw)
    cum_t = running_t(raw)
    shifted = cum - jnp.concatenate(log_step, axis=0)

    def red_copy(j, half):
        rows = pl.ds(half * PIECE, PIECE)
        return remote(
            mid.at[j, rows, :], red.at[z, rows, :],
            S_RED + 2 * j + half, R_RED + 2 * z + half, 2 * j + k, c,
        )

    def log_copy(j):
        return remote(midlog.at[j], redlog.at[z], S_LOG + j, R_LOG + z, 2 * j + k, c)

    for j in range(CHIPS):
        @pl.when(no(both(mid_self, c // 2 == j)))
        def _():
            arrived(midlog.at[j], R_MLOG + j)

        @pl.when(z != j)
        def _():
            log_copy(j).start()

        @pl.when(z == j)
        def _():
            redlog[z] = midlog[j]

    for half in range(HALVES):
        rows = pl.ds(half * PIECE, PIECE)
        for j in range(CHIPS):
            @pl.when(no(both(mid_self, c // 2 == j)))
            def _():
                arrived(mid.at[j, rows, :], R_MID + 2 * j + half)

            @pl.when(z != j)
            def _():
                red_copy(j, half).start()

            @pl.when(z == j)
            def _():
                red[z, rows, :] = mid[j, rows, :]

    @pl.when(p != c)
    def _():
        arrived(tx, R_TAIL)

    @pl.when(p < ROWS - 1)
    def _():
        arrived(tbc, R_TAIL + 1)

    for slot in range(2):
        xcv[slot, :16, :] = causal_conv(cx[slot, :16, :], tx[...], wcx[...].astype(F32)).astype(BF16)
        for which in range(2):
            bcv[which, slot, :16, :] = causal_conv(
                cbc[which, slot, :16, :], tbc[which], wcbc[which].astype(F32)
            ).astype(BF16)
        scores[slot] = dot_nt(bcv[1, slot], bcv[0, slot])

    lane_low = lax.broadcasted_iota(jnp.int32, (TOK, 128), 1) < HEAD_WIDTH
    causal = (
        lax.broadcasted_iota(jnp.int32, (128, 128), 1) <= lax.broadcasted_iota(jnp.int32, (128, 128), 0)
    )

    def intra(slot, pair):
        cols = pl.ds(pair * 128, 128)
        x = xcv[slot, :, cols]
        made = []
        spread_logs = []
        for h in (2 * pair, 2 * pair + 1):
            at = slot * 16 + h
            down = jnp.broadcast_to(cum_t[:, at : at + 1], (TOK, 128))
            left = down - shifted[at : at + 1, :128]
            right = down[128:] - shifted[at : at + 1, 128:]
            top = jnp.exp2(jnp.where(causal, left[:128], -jnp.inf)) * scores[slot, :128, :128]
            low = jnp.exp2(left[128:]) * scores[slot, 128:, :128]
            diag = jnp.exp2(jnp.where(causal, right, -jnp.inf)) * scores[slot, 128:, 128:]
            y0 = jnp.dot(top.astype(BF16), x[:128], preferred_element_type=F32)
            y1 = jnp.dot(low.astype(BF16), x[:128], preferred_element_type=F32) + jnp.dot(
                diag.astype(BF16), x[128:], preferred_element_type=F32
            )
            made.append(jnp.concatenate([y0, y1], axis=0))
            spread_logs.append(down)
        g = silu(cg[slot, :, cols].astype(F32))
        part[slot, :, cols] = jnp.where(lane_low, made[0], made[1]) * g
        coef[slot, :, cols] = jnp.exp2(jnp.where(lane_low, spread_logs[0], spread_logs[1])) * g

    work = [(slot, pair) for slot in range(2) for pair in range(8)]
    for slot, pair in work[:10]:
        intra(slot, pair)

    for chip in range(CHIPS):
        @pl.when(z != chip)
        def _():
            arrived(redlog.at[chip], R_LOG + chip)

    later = jnp.zeros((1, 128), F32)
    scales = []
    for chip in range(CHIPS - 1, -1, -1):
        scales.insert(0, jnp.exp2(later)[:, :1])
        later = later + redlog[chip]

    def mine(half):
        return ds(c * HEAD_WIDTH + half * PIECE, PIECE)

    def ag_copy(step, half):
        return remote(
            stf.at[mine(half), :], stf.at[mine(half), :],
            S_AG + HALVES * (step - 1) + half, R_AG + HALVES * c + half, p, lax.rem(c + step, COLS),
        )

    for half in range(HALVES):
        rows = pl.ds(half * PIECE, PIECE)
        for chip in range(CHIPS):
            @pl.when(z != chip)
            def _():
                arrived(red.at[chip, rows, :], R_RED + 2 * chip + half)

        state = None
        for chip in range(CHIPS):
            term = red[chip, rows, :].astype(F32) * scales[chip]
            state = term if state is None else state + term
        stf[mine(half), :] = state.astype(BF16)
        for step in range(1, COLS):
            ag_copy(step, half).start()
        for slot, pair in work[10 + 3 * half : 13 + 3 * half]:
            intra(slot, pair)

    for copy in sib_copies:
        copy.wait_send()

    @pl.when(halo_out)
    def _():
        for copy in halo_copies():
            copy.wait_send()

    @pl.when(tail_out)
    def _():
        tail_copy().wait_send()

    @pl.when(p == c)
    def _():
        for step in range(1, COLS):
            relay_copy(step).wait_send()

    @pl.when(p == ROWS - 1)
    def _():
        for j in range(ROWS - 1):
            tail_bc(j).wait_send()

    for i in range(8):
        @pl.when(no(mid_own(i)))
        def _():
            mlog_copy(i).wait_send()
            for half in range(HALVES):
                mid_copy(i, half).wait_send()

    for half in range(HALVES):
        for j in range(CHIPS):
            @pl.when(z != j)
            def _():
                red_copy(j, half).wait_send()
                if half == 0:
                    log_copy(j).wait_send()

    def sq_copy(slot):
        return remote(sq.at[slot], sqs.at[slot], S_SQ + slot, R_SQ + slot, sib, c)

    for chunk in range(4):
        for source in range(4 * chunk, 4 * chunk + 4):
            @pl.when(c != source)
            def _():
                for half in range(HALVES):
                    arrived(
                        stf.at[pl.ds(source * HEAD_WIDTH + half * PIECE, PIECE), :],
                        R_AG + HALVES * source + half,
                    )

        cols = pl.ds(chunk * 256, 256)
        for slot in range(2):
            read = dot_nt(bcv[1, slot], stf[cols, :])
            gated = part[slot, :, cols] + coef[slot, :, cols] * read
            part[slot, :, cols] = gated
            squares = gated[:, :128] * gated[:, :128] + gated[:, 128:] * gated[:, 128:]
            sq[slot] = squares if chunk == 0 else sq[slot] + squares
            if chunk == 3:
                sq_copy(slot).start()

    for half in range(HALVES):
        for step in range(1, COLS):
            ag_copy(step, half).wait_send()
    copies[L_GAIN].wait()
    copies[L_LEN].wait()
    gains = gain[...]
    position = lax.broadcasted_iota(jnp.int32, (TOK, 1), 0)
    outs = []
    for slot in range(2):
        arrived(sqs.at[slot], R_SQ + slot)
        mean = jnp.sum(sq[slot] + sqs[slot], axis=1, keepdims=True) * (1.0 / (GROUP_HEADS * HEAD_WIDTH))
        scale = jnp.where(position < slen[slot], lax.rsqrt(mean + EPS), 0.0)
        obuf[slot] = (part[slot] * scale * gains).astype(BF16)
        copy = pltpu.make_async_copy(obuf.at[slot], out.at[slot], lsem.at[L_OUT + slot])
        copy.start()
        outs.append(copy)

    for slot in range(2):
        sq_copy(slot).wait_send()
    for copy in outs:
        copy.wait()


def local(
    prompt_inner,
    prompt_proj,
    prompt_step,
    completion_inner,
    completion_gate,
    completion_projections,
    sample_step,
    sample_length,
    decay_log,
    conv_inner,
    conv_proj,
    norm_gain,
):
    hbm = pl.BlockSpec(memory_space=pl.ANY)
    V = pltpu.VMEM
    layer = pl.pallas_call(
        kernel,
        out_shape=jax.ShapeDtypeStruct(completion_inner.shape, BF16),
        in_specs=[hbm] * 12,
        out_specs=hbm,
        scratch_shapes=[
            V((2, TOK, HALF), BF16),
            V((2, TOK, STATE_WIDTH), BF16),
            V((2, 8, TOK), F32),
            V((EDGE, HALF), BF16),
            V((EDGE, STATE_WIDTH), BF16),
            V((CONV, HALF), BF16),
            V((CONV, STATE_WIDTH), BF16),
            V((2, TOK, FEAT), BF16),
            V((2, TOK, FEAT), BF16),
            V((2, 2, TOK, STATE_WIDTH), BF16),
            V((16, 2, TOK), F32),
            V((CONV, FEAT), BF16),
            V((2, CONV, STATE_WIDTH), BF16),
            V((EDGE, FEAT), BF16),
            V((2, EDGE, STATE_WIDTH), BF16),
            V((EDGE, 2 * PROJ_C), BF16),
            V((STATE_GROUPS, 2, EDGE, STATE_WIDTH), BF16),
            V((2, TOK, HALF), BF16),
            V((2, TOK, HALF), F32),
            V((2, TOK, STATE_WIDTH), BF16),
            V((HALF, STATE_WIDTH), F32),
            V((HALF, STATE_WIDTH), BF16),
            V((8, 1, 128), F32),
            V((CHIPS, 1, 128), F32),
            V((CHIPS, 1, 128), F32),
            V((CHIPS, HEAD_WIDTH, STATE_WIDTH), BF16),
            V((CHIPS, HEAD_WIDTH, STATE_WIDTH), BF16),
            V((FEAT, STATE_WIDTH), BF16),
            V((2, TOK, FEAT), BF16),
            V((2, 2, TOK, STATE_WIDTH), BF16),
            V((2, TOK, FEAT), F32),
            V((2, TOK, FEAT), F32),
            V((2, TOK, TOK), F32),
            V((2, TOK, 128), F32),
            V((2, TOK, 128), F32),
            V((2, TOK, FEAT), BF16),
            pltpu.SMEM((2,), jnp.int32),
            V((1, STATE_HEADS), F32),
            V((1, FEAT), F32),
            pltpu.SemaphoreType.DMA((N_LOCAL,)),
            pltpu.SemaphoreType.DMA((N_SEND,)),
            pltpu.SemaphoreType.DMA((N_RECV,)),
        ],
        compiler_params=pltpu.CompilerParams(
            collective_id=0, has_side_effects=True, vmem_limit_bytes=48 << 20
        ),
        name="layer",
    )
    arrays = (
        prompt_inner,
        prompt_proj,
        prompt_step,
        completion_inner,
        completion_gate,
        completion_projections,
        sample_step,
        sample_length,
        decay_log.reshape(1, STATE_HEADS),
        conv_inner,
        conv_proj,
        norm_gain.reshape(1, FEAT),
    )
    return layer(*[pltpu.with_memory_space_constraint(array, pltpu.HBM) for array in arrays])


def solution(mesh):
    placed = (
        P("prompt", "comp"),
        P("prompt", None),
        P("comp", "prompt"),
        P("comp", None, "prompt"),
        P("comp", None, "prompt"),
        P("comp", None, None),
        P("prompt", "comp", None),
        P("comp"),
        P(),
        P(),
        P(),
        P("prompt"),
    )
    return jax.shard_map(
        local, mesh=mesh, in_specs=placed, out_specs=P("comp", None, "prompt"), check_vma=False
    )
```

```python
import functools

import jax
import jax.numpy as jnp
from jax import lax
from jax.experimental import pallas as pl
from jax.experimental.pallas import tpu as pltpu
from jax.sharding import PartitionSpec as P

STATE_HEADS = 256
HEAD_WIDTH = 64
STATE_WIDTH = 256
STATE_GROUPS = 8
CONV = 4
EPS = 1e-05
LOG2E = 1.4426950408889634

MESH = pl.DeviceIdType.MESH
F32 = jnp.float32
BF16 = jnp.bfloat16

ROWS = 16
COLS = 16
CHIPS = 8
TOK = 256
FEAT = 1024
HALF = 512
GROUP_HEADS = 32
PROJ_C = STATE_GROUPS * STATE_WIDTH

EDGE = 8
HALVES = 2
PIECES = ((0, 16), (16, 48))

R_SIB, R_HALO, R_TAIL, R_MLOG, R_LOG, R_MID = 0, 3, 5, 7, 15, 23
R_RED = R_MID + CHIPS * HALVES
R_AG = R_RED + CHIPS * HALVES
R_SQ = R_AG + COLS * HALVES
N_RECV = R_SQ + 2
S_SIB, S_HALO, S_TX, S_RELAY, S_TB = 0, 3, 7, 8, 23
S_MLOG = S_TB + 15
S_LOG = S_MLOG + 8
S_MID = S_LOG + 8
S_RED = S_MID + CHIPS * HALVES
S_AG = S_RED + CHIPS * HALVES
S_SQ = S_AG + (COLS - 1) * HALVES
N_SEND = S_SQ + 2
(L_PX, L_PB, L_PS, L_WX, L_WB, L_CX, L_CG, L_CB, L_CC, L_SS, L_WCX, L_WCB, L_WCC, L_TX, L_TB, L_TC, L_LEN, L_LOG, L_GAIN, L_OUT) = range(20)
N_LOCAL = 21


def silu(v):
    h = 0.5 * v
    return h + h * jnp.tanh(h)


def softplus(v):
    return jnp.maximum(v, 0.0) + jnp.log1p(jnp.exp(-jnp.abs(v)))


def split3(v):
    a = v.astype(BF16)
    r = v - a.astype(F32)
    b = r.astype(BF16)
    c = (r - b.astype(F32)).astype(BF16)
    return a, b, c


def dot_nt(a, b):
    return lax.dot_general(a, b, (((1,), (1,)), ((), ())), preferred_element_type=F32)


def dot_tn(a, b):
    return lax.dot_general(a, b, (((0,), (0,)), ((), ())), preferred_element_type=F32)


def convolve(x, taps):
    total = x * taps[3:4]
    for lag in (1, 2, 3):
        total = total + pltpu.roll(x, lag, 0) * taps[3 - lag : 4 - lag]
    return silu(total)


def causal_conv(src, lead, taps):
    return convolve(jnp.concatenate([lead.astype(F32), src.astype(F32)], axis=0), taps)[EDGE:]


def pick_rows(row, first, count):
    lanes = lax.broadcasted_iota(jnp.int32, (count, row.shape[1]), 1)
    heads = first + lax.broadcasted_iota(jnp.int32, (count, row.shape[1]), 0)
    wide = jnp.broadcast_to(row, (count, row.shape[1]))
    return jnp.sum(jnp.where(lanes == heads, wide, 0.0), axis=1, keepdims=True)


def kernel(
    inner, proj, pstep, cin, gate, cproj, sstep, slen_in, dlog_in, cvi, cvp, gain_in, out,
    px, pb, ps, hx, hb, wx, wb, cx, cg, cbc, ss, wcx, wcbc, tx, tbc,
    trow, tpack, xw, wide, bb, base, st, logs, midlog, redlog, mid, red, stf, xcv, bcv, part, coef, scores, sq, sqs, obuf,
    slen, dlog, gain, lsem, ssem, rsem,
):
    p = lax.axis_index("prompt")
    c = lax.axis_index("comp")
    z = p // 2
    k = p % 2
    other = 1 - k
    sib = p + 1 - 2 * k
    group_col = c // 2
    group_row = p // 2
    kk = c // 8
    c_core = c % 2
    no = jnp.logical_not
    both = jnp.logical_and

    def ds(start, size):
        return pl.ds(pl.multiple_of(start, size), size)

    def local(src, dst, sem):
        copy = pltpu.make_async_copy(src, dst, lsem.at[sem])
        copy.start()
        return copy

    def remote(src, dst, send, recv, row, col):
        return pltpu.make_async_remote_copy(
            src_ref=src, dst_ref=dst, send_sem=ssem.at[send], recv_sem=rsem.at[recv],
            device_id=(row, col), device_id_type=MESH,
        )

    def arrived(dst, recv):
        remote(dst, dst, 0, recv, p, c).wait_recv()

    barrier = pltpu.get_barrier_semaphore()

    def greet(row, col):
        pl.semaphore_signal(barrier, inc=1, device_id=(row, col), device_id_type=MESH)

    tail_self = both(p == ROWS - 1, c == COLS - 1)
    mid_self = both(kk == k, c_core == k)
    for step in (4, 3, 5, 2, 6, 1, 7):
        greet(lax.rem(p + 2 * step, ROWS), c)

    @pl.when(z > 0)
    def _():
        greet(2 * z - 1, c)

    @pl.when(both(p == c, p < ROWS - 1))
    def _():
        greet(ROWS - 1, c)

    @pl.when(p < ROWS - 1)
    def _():
        greet(ROWS - 1, c)

    for j in range(CHIPS):
        @pl.when(no(both(mid_self, c // 2 == j)))
        def _():
            greet(2 * z + kk, 2 * j + k)

    for step in range(1, COLS):
        greet(p, lax.rem(c + step, COLS))

    greet(sib, c)

    b_col = group_col * STATE_WIDTH
    b_row = group_row * STATE_WIDTH
    copies = {}
    copies[L_LOG] = local(dlog_in, dlog, L_LOG)
    copies[L_PS] = local(pstep.at[ds(8 * k, 8), :], ps.at[k], L_PS)
    copies[L_PB] = local(proj.at[:, ds(b_col, STATE_WIDTH)], pb.at[k], L_PB)
    copies[L_WB] = local(cvp.at[:, ds(b_col, STATE_WIDTH)], wb, L_WB)
    copies[L_PX] = local(inner.at[:, ds(k * HALF, HALF)], px.at[k], L_PX)
    copies[L_WX] = local(cvi.at[:, ds(c * FEAT + k * HALF, HALF)], wx, L_WX)

    last_row = (p == ROWS - 1).astype(jnp.int32)
    halo_out = both(k == 1, p < ROWS - 1)
    expected = (
        1 + 2 * halo_out.astype(jnp.int32)
        + CHIPS - mid_self.astype(jnp.int32) + CHIPS - 1 + COLS - 1
        + last_row * ROWS - tail_self.astype(jnp.int32)
    )
    pl.semaphore_wait(barrier, expected)

    edge_rows = pl.ds(TOK - EDGE, EDGE)
    sib_copies = [
        remote(pstep.at[ds(8 * other, 8), :], ps.at[k], S_SIB, R_SIB, sib, c),
        remote(proj.at[:, ds(b_col, STATE_WIDTH)], pb.at[k], S_SIB + 1, R_SIB + 1, sib, c),
        remote(inner.at[:, ds(other * HALF, HALF)], px.at[k], S_SIB + 2, R_SIB + 2, sib, c),
    ]

    def halo_copies():
        found = []
        for core in range(2):
            found.append(
                remote(
                    inner.at[edge_rows, pl.ds(core * HALF, HALF)], hx,
                    S_HALO + 2 * core, R_HALO, p + 1 + core, c,
                )
            )
            found.append(
                remote(
                    proj.at[edge_rows, ds(b_col, STATE_WIDTH)], hb,
                    S_HALO + 2 * core + 1, R_HALO + 1, p + 1 + core, c,
                )
            )
        return found

    @pl.when(halo_out)
    def _():
        for copy in halo_copies():
            copy.start()

    for copy in sib_copies:
        copy.start()

    @pl.when(z == 0)
    def _():
        hx[...] = jnp.zeros_like(hx)
        hb[...] = jnp.zeros_like(hb)

    def tail_copy():
        return remote(inner.at[edge_rows, :], tx, S_TX, R_TAIL, c, c)

    def relay_copy(step):
        return remote(tx, tx, S_RELAY + step - 1, R_TAIL, p, lax.rem(c + step, COLS))

    def tail_bc(j):
        return remote(tpack.at[j // 2], tbc, S_TB + j, R_TAIL + 1, j, c)

    def tail_local():
        return pltpu.make_async_copy(inner.at[edge_rows, :], tx, lsem.at[L_TX])

    def tail_proj():
        return pltpu.make_async_copy(proj.at[edge_rows, :], trow, lsem.at[L_TB])

    tail_out = both(p == ROWS - 1, c < COLS - 1)

    @pl.when(tail_out)
    def _():
        tail_copy().start()

    @pl.when(tail_self)
    def _():
        tail_local().start()

    @pl.when(p == ROWS - 1)
    def _():
        tail_proj().start()

    copies[L_SS] = local(sstep, ss, L_SS)
    copies[L_CX] = local(cin, cx, L_CX)
    copies[L_WCX] = local(cvi.at[:, ds(p * FEAT, FEAT)], wcx, L_WCX)
    copies[L_CB] = local(cproj.at[:, :, ds(b_row, STATE_WIDTH)], cbc.at[0], L_CB)
    copies[L_CC] = local(cproj.at[:, :, ds(PROJ_C + b_row, STATE_WIDTH)], cbc.at[1], L_CC)
    copies[L_WCB] = local(cvp.at[:, ds(b_row, STATE_WIDTH)], wcbc.at[0], L_WCB)
    copies[L_WCC] = local(cvp.at[:, ds(PROJ_C + b_row, STATE_WIDTH)], wcbc.at[1], L_WCC)
    copies[L_CG] = local(gate, cg, L_CG)
    copies[L_GAIN] = local(gain_in, gain, L_GAIN)
    copies[L_LEN] = local(slen_in, slen, L_LEN)

    row_id = lax.broadcasted_iota(jnp.int32, (TOK, TOK), 0)
    col_id = lax.broadcasted_iota(jnp.int32, (TOK, TOK), 1)
    tri = jnp.where(col_id <= row_id, 1.0, 0.0).astype(BF16)

    def running(values):
        a, b, d = split3(values)
        return dot_nt(a, tri) + (dot_nt(b, tri) + dot_nt(d, tri))

    def running_t(values):
        a, b, d = split3(values)
        return dot_nt(tri, a) + (dot_nt(tri, b) + dot_nt(tri, d))

    copies[L_LOG].wait()
    rate_col = jnp.exp(pick_rows(dlog[...], c * 16 + 8 * k, 8)) * LOG2E
    spread = jnp.where(
        lax.broadcasted_iota(jnp.int32, (24, HALF), 1) // HEAD_WIDTH
        == lax.broadcasted_iota(jnp.int32, (24, HALF), 0) % 8,
        1.0,
        0.0,
    ).astype(BF16)

    def weigh(block):
        dt = softplus(ps[block])
        run = running(-rate_col * dt)
        total = run[:, TOK - 1 :]
        weight = jnp.exp2(total - run) * dt
        pieces = jnp.concatenate([piece.astype(F32) for piece in split3(weight)], axis=0).astype(BF16)
        wide[block] = dot_tn(pieces, spread)
        return total

    def conv_b(block):
        x = pb[block].astype(F32)
        bb[block] = convolve(x, wb[...].astype(F32)).astype(BF16)

    def conv_x(block):
        for quarter in range(4):
            cols = pl.ds(quarter * 128, 128)
            x = px[block, :, cols].astype(F32)
            xw[block, :, cols] = (convolve(x, wx[:, cols].astype(F32)) * wide[block, :, cols]).astype(BF16)

    copies[L_PS].wait()
    total_own = weigh(k)
    copies[L_PB].wait()
    copies[L_WB].wait()
    conv_b(k)
    copies[L_PX].wait()
    copies[L_WX].wait()
    conv_x(k)

    @pl.when(p == ROWS - 1)
    def _():
        tail_proj().wait()
        for group in range(STATE_GROUPS):
            for which in range(2):
                first = which * PROJ_C + group * STATE_WIDTH
                tpack[group, which] = trow[:, first : first + STATE_WIDTH]
        tbc[...] = tpack[group_row]
        for j in range(ROWS - 1):
            tail_bc(j).start()

    arrived(ps.at[other], R_SIB)
    total_sib = weigh(other)
    total1 = jnp.where(k == 1, total_own, total_sib)
    total_chip = jnp.broadcast_to(total_own + total_sib, (8, 128))
    for i in range(8):
        logs[i] = total_chip[i : i + 1]

    def mid_own(i):
        return both(mid_self, 8 * k + i == c)

    def mlog_copy(i):
        return remote(
            logs.at[i], midlog.at[c // 2], S_MLOG + i, R_MLOG + c // 2, 2 * z + c_core, 8 * k + i
        )

    for i in range(8):
        @pl.when(no(mid_own(i)))
        def _():
            mlog_copy(i).start()

        @pl.when(mid_own(i))
        def _():
            midlog[c // 2] = logs[i]

    arrived(pb.at[other], R_SIB + 1)
    arrived(px.at[other], R_SIB + 2)
    conv_b(other)
    conv_x(other)

    taps_b = wb[...].astype(F32)
    taps_x = wx[...].astype(F32)
    bb[1, :16, :] = causal_conv(pb[1, :16, :], pb[0, edge_rows, :], taps_b).astype(BF16)
    xw[1, :16, :] = (causal_conv(px[1, :16, :], px[0, edge_rows, :], taps_x) * wide[1, :16, :]).astype(BF16)
    xw[0, :16, :] = jnp.zeros((16, HALF), BF16)
    decay1 = jnp.exp2(jnp.broadcast_to(total1, (8, STATE_WIDTH)))
    for pair in range(4):
        cols = pl.ds(pair * 128, 128)
        first = dot_tn(xw[0, :, cols], bb[0])
        second = dot_tn(xw[1, :, cols], bb[1])
        for side in range(2):
            i = 2 * pair + side
            rows = slice(side * HEAD_WIDTH, (side + 1) * HEAD_WIDTH)
            base[pl.ds(i * HEAD_WIDTH, HEAD_WIDTH), :] = first[rows] * decay1[i : i + 1] + second[rows]

    @pl.when(z > 0)
    def _():
        arrived(hx, R_HALO)
        arrived(hb, R_HALO + 1)

    edge_b = causal_conv(pb[0, :16, :], hb[...], taps_b).astype(BF16)
    edge_x = (causal_conv(px[0, :16, :], hx[...], taps_x) * wide[0, :16, :]).astype(BF16)

    def mid_copy(i, half):
        first, count = PIECES[half]
        rows = pl.ds(i * HEAD_WIDTH + first, count)
        return remote(
            st.at[rows, :], mid.at[c // 2, pl.ds(first, count), :],
            S_MID + 2 * i + half, R_MID + 2 * (c // 2) + half, 2 * z + c_core, 8 * k + i,
        )

    for pair in range(4):
        edge = dot_tn(edge_x[:, pair * 128 : pair * 128 + 128], edge_b)
        for side in range(2):
            i = 2 * pair + side
            rows = slice(side * HEAD_WIDTH, (side + 1) * HEAD_WIDTH)
            mine_i = pl.ds(i * HEAD_WIDTH, HEAD_WIDTH)
            st[mine_i, :] = (base[mine_i, :] + edge[rows] * decay1[i : i + 1]).astype(BF16)

            @pl.when(no(mid_own(i)))
            def _():
                mid_copy(i, 0).start()

            @pl.when(mid_own(i))
            def _():
                mid[c // 2] = st[pl.ds(i * HEAD_WIDTH, HEAD_WIDTH), :]

    for half in range(1, HALVES):
        for i in range(8):
            @pl.when(no(mid_own(i)))
            def _():
                mid_copy(i, half).start()

    @pl.when(both(p == c, no(tail_self)))
    def _():
        arrived(tx, R_TAIL)

    @pl.when(tail_self)
    def _():
        tail_local().wait()

    @pl.when(p == c)
    def _():
        for step in range(1, COLS):
            relay_copy(step).start()

    copies[L_CB].wait()
    copies[L_CC].wait()
    copies[L_WCB].wait()
    copies[L_WCC].wait()
    copies[L_WCX].wait()
    copies[L_CX].wait()
    copies[L_CG].wait()
    for slot in range(2):
        for eighth in range(8):
            cols = pl.ds(eighth * 128, 128)
            x = cx[slot, :, cols].astype(F32)
            xcv[slot, :, cols] = convolve(x, wcx[:, cols].astype(F32)).astype(BF16)
        for which in range(2):
            x = cbc[which, slot].astype(F32)
            bcv[which, slot] = convolve(x, wcbc[which].astype(F32)).astype(BF16)

    copies[L_SS].wait()
    rate_row = jnp.exp(pick_rows(dlog[...], p * 16, 16)) * LOG2E
    log_step = []
    raw = []
    for slot in range(2):
        dt = softplus(ss[:, slot, :])
        raw.append(-rate_row * dt)
        log_step.append(jnp.log2(dt))
    raw = jnp.concatenate(raw, axis=0)
    cum = running(raw)
    cum_t = running_t(raw)
    shifted = cum - jnp.concatenate(log_step, axis=0)

    def red_copy(j, half):
        rows = pl.ds(*PIECES[half])
        return remote(
            mid.at[j, rows, :], red.at[z, rows, :],
            S_RED + 2 * j + half, R_RED + 2 * z + half, 2 * j + k, c,
        )

    def log_copy(j):
        return remote(midlog.at[j], redlog.at[z], S_LOG + j, R_LOG + z, 2 * j + k, c)

    for j in range(CHIPS):
        @pl.when(no(both(mid_self, c // 2 == j)))
        def _():
            arrived(midlog.at[j], R_MLOG + j)

        @pl.when(z != j)
        def _():
            log_copy(j).start()

        @pl.when(z == j)
        def _():
            redlog[z] = midlog[j]

    for half in range(HALVES):
        rows = pl.ds(*PIECES[half])
        for j in range(CHIPS):
            @pl.when(no(both(mid_self, c // 2 == j)))
            def _():
                arrived(mid.at[j, rows, :], R_MID + 2 * j + half)

            @pl.when(z != j)
            def _():
                red_copy(j, half).start()

            @pl.when(z == j)
            def _():
                red[z, rows, :] = mid[j, rows, :]

    @pl.when(p != c)
    def _():
        arrived(tx, R_TAIL)

    @pl.when(p < ROWS - 1)
    def _():
        arrived(tbc, R_TAIL + 1)

    for slot in range(2):
        xcv[slot, :16, :] = causal_conv(cx[slot, :16, :], tx[...], wcx[...].astype(F32)).astype(BF16)
        for which in range(2):
            bcv[which, slot, :16, :] = causal_conv(
                cbc[which, slot, :16, :], tbc[which], wcbc[which].astype(F32)
            ).astype(BF16)
        scores[slot] = dot_nt(bcv[1, slot], bcv[0, slot])

    lane_low = lax.broadcasted_iota(jnp.int32, (TOK, 128), 1) < HEAD_WIDTH
    causal = (
        lax.broadcasted_iota(jnp.int32, (128, 128), 1) <= lax.broadcasted_iota(jnp.int32, (128, 128), 0)
    )

    def intra(slot, pair):
        cols = pl.ds(pair * 128, 128)
        x = xcv[slot, :, cols]
        made = []
        spread_logs = []
        for h in (2 * pair, 2 * pair + 1):
            at = slot * 16 + h
            down = jnp.broadcast_to(cum_t[:, at : at + 1], (TOK, 128))
            left = down - shifted[at : at + 1, :128]
            right = down[128:] - shifted[at : at + 1, 128:]
            top = jnp.exp2(jnp.where(causal, left[:128], -jnp.inf)) * scores[slot, :128, :128]
            low = jnp.exp2(left[128:]) * scores[slot, 128:, :128]
            diag = jnp.exp2(jnp.where(causal, right, -jnp.inf)) * scores[slot, 128:, 128:]
            y0 = jnp.dot(top.astype(BF16), x[:128], preferred_element_type=F32)
            y1 = jnp.dot(low.astype(BF16), x[:128], preferred_element_type=F32) + jnp.dot(
                diag.astype(BF16), x[128:], preferred_element_type=F32
            )
            made.append(jnp.concatenate([y0, y1], axis=0))
            spread_logs.append(down)
        g = silu(cg[slot, :, cols].astype(F32))
        part[slot, :, cols] = jnp.where(lane_low, made[0], made[1]) * g
        coef[slot, :, cols] = jnp.exp2(jnp.where(lane_low, spread_logs[0], spread_logs[1])) * g

    work = [(slot, pair) for slot in range(2) for pair in range(8)]
    for slot, pair in work[:10]:
        intra(slot, pair)

    for chip in range(CHIPS):
        @pl.when(z != chip)
        def _():
            arrived(redlog.at[chip], R_LOG + chip)

    later = jnp.zeros((1, 128), F32)
    scales = []
    for chip in range(CHIPS - 1, -1, -1):
        scales.insert(0, jnp.exp2(later)[:, :1])
        later = later + redlog[chip]

    def mine(half):
        first, count = PIECES[half]
        return pl.ds(pl.multiple_of(c * HEAD_WIDTH + first, 16), count)

    def ag_copy(step, half):
        return remote(
            stf.at[mine(half), :], stf.at[mine(half), :],
            S_AG + HALVES * (step - 1) + half, R_AG + HALVES * c + half, p, lax.rem(c + step, COLS),
        )

    for half in range(HALVES):
        rows = pl.ds(*PIECES[half])
        for chip in range(CHIPS):
            @pl.when(z != chip)
            def _():
                arrived(red.at[chip, rows, :], R_RED + 2 * chip + half)

        state = None
        for chip in range(CHIPS):
            term = red[chip, rows, :].astype(F32) * scales[chip]
            state = term if state is None else state + term
        stf[mine(half), :] = state.astype(BF16)
        for step in range(1, COLS):
            ag_copy(step, half).start()
        for slot, pair in work[10 + 3 * half : 13 + 3 * half]:
            intra(slot, pair)

    for copy in sib_copies:
        copy.wait_send()

    @pl.when(halo_out)
    def _():
        for copy in halo_copies():
            copy.wait_send()

    @pl.when(tail_out)
    def _():
        tail_copy().wait_send()

    @pl.when(p == c)
    def _():
        for step in range(1, COLS):
            relay_copy(step).wait_send()

    @pl.when(p == ROWS - 1)
    def _():
        for j in range(ROWS - 1):
            tail_bc(j).wait_send()

    for i in range(8):
        @pl.when(no(mid_own(i)))
        def _():
            mlog_copy(i).wait_send()
            for half in range(HALVES):
                mid_copy(i, half).wait_send()

    for half in range(HALVES):
        for j in range(CHIPS):
            @pl.when(z != j)
            def _():
                red_copy(j, half).wait_send()
                if half == 0:
                    log_copy(j).wait_send()

    def sq_copy(slot):
        return remote(sq.at[slot], sqs.at[slot], S_SQ + slot, R_SQ + slot, sib, c)

    for chunk in range(4):
        for source in range(4 * chunk, 4 * chunk + 4):
            @pl.when(c != source)
            def _():
                for half in range(HALVES):
                    arrived(
                        stf.at[pl.ds(source * HEAD_WIDTH + PIECES[half][0], PIECES[half][1]), :],
                        R_AG + HALVES * source + half,
                    )

        cols = pl.ds(chunk * 256, 256)
        for slot in range(2):
            read = dot_nt(bcv[1, slot], stf[cols, :])
            gated = part[slot, :, cols] + coef[slot, :, cols] * read
            part[slot, :, cols] = gated
            squares = gated[:, :128] * gated[:, :128] + gated[:, 128:] * gated[:, 128:]
            sq[slot] = squares if chunk == 0 else sq[slot] + squares
            if chunk == 3:
                sq_copy(slot).start()

    for half in range(HALVES):
        for step in range(1, COLS):
            ag_copy(step, half).wait_send()
    copies[L_GAIN].wait()
    copies[L_LEN].wait()
    gains = gain[...]
    position = lax.broadcasted_iota(jnp.int32, (TOK, 1), 0)
    outs = []
    for slot in range(2):
        arrived(sqs.at[slot], R_SQ + slot)
        mean = jnp.sum(sq[slot] + sqs[slot], axis=1, keepdims=True) * (1.0 / (GROUP_HEADS * HEAD_WIDTH))
        scale = jnp.where(position < slen[slot], lax.rsqrt(mean + EPS), 0.0)
        obuf[slot] = (part[slot] * scale * gains).astype(BF16)
        copy = pltpu.make_async_copy(obuf.at[slot], out.at[slot], lsem.at[L_OUT + slot])
        copy.start()
        outs.append(copy)

    for slot in range(2):
        sq_copy(slot).wait_send()
    for copy in outs:
        copy.wait()


def local(
    prompt_inner,
    prompt_proj,
    prompt_step,
    completion_inner,
    completion_gate,
    completion_projections,
    sample_step,
    sample_length,
    decay_log,
    conv_inner,
    conv_proj,
    norm_gain,
):
    hbm = pl.BlockSpec(memory_space=pl.ANY)
    V = pltpu.VMEM
    layer = pl.pallas_call(
        kernel,
        out_shape=jax.ShapeDtypeStruct(completion_inner.shape, BF16),
        in_specs=[hbm] * 12,
        out_specs=hbm,
        scratch_shapes=[
            V((2, TOK, HALF), BF16),
            V((2, TOK, STATE_WIDTH), BF16),
            V((2, 8, TOK), F32),
            V((EDGE, HALF), BF16),
            V((EDGE, STATE_WIDTH), BF16),
            V((CONV, HALF), BF16),
            V((CONV, STATE_WIDTH), BF16),
            V((2, TOK, FEAT), BF16),
            V((2, TOK, FEAT), BF16),
            V((2, 2, TOK, STATE_WIDTH), BF16),
            V((16, 2, TOK), F32),
            V((CONV, FEAT), BF16),
            V((2, CONV, STATE_WIDTH), BF16),
            V((EDGE, FEAT), BF16),
            V((2, EDGE, STATE_WIDTH), BF16),
            V((EDGE, 2 * PROJ_C), BF16),
            V((STATE_GROUPS, 2, EDGE, STATE_WIDTH), BF16),
            V((2, TOK, HALF), BF16),
            V((2, TOK, HALF), F32),
            V((2, TOK, STATE_WIDTH), BF16),
            V((HALF, STATE_WIDTH), F32),
            V((HALF, STATE_WIDTH), BF16),
            V((8, 1, 128), F32),
            V((CHIPS, 1, 128), F32),
            V((CHIPS, 1, 128), F32),
            V((CHIPS, HEAD_WIDTH, STATE_WIDTH), BF16),
            V((CHIPS, HEAD_WIDTH, STATE_WIDTH), BF16),
            V((FEAT, STATE_WIDTH), BF16),
            V((2, TOK, FEAT), BF16),
            V((2, 2, TOK, STATE_WIDTH), BF16),
            V((2, TOK, FEAT), F32),
            V((2, TOK, FEAT), F32),
            V((2, TOK, TOK), F32),
            V((2, TOK, 128), F32),
            V((2, TOK, 128), F32),
            V((2, TOK, FEAT), BF16),
            pltpu.SMEM((2,), jnp.int32),
            V((1, STATE_HEADS), F32),
            V((1, FEAT), F32),
            pltpu.SemaphoreType.DMA((N_LOCAL,)),
            pltpu.SemaphoreType.DMA((N_SEND,)),
            pltpu.SemaphoreType.DMA((N_RECV,)),
        ],
        compiler_params=pltpu.CompilerParams(
            collective_id=0, has_side_effects=True, vmem_limit_bytes=48 << 20
        ),
        name="layer",
    )
    arrays = (
        prompt_inner,
        prompt_proj,
        prompt_step,
        completion_inner,
        completion_gate,
        completion_projections,
        sample_step,
        sample_length,
        decay_log.reshape(1, STATE_HEADS),
        conv_inner,
        conv_proj,
        norm_gain.reshape(1, FEAT),
    )
    return layer(*[pltpu.with_memory_space_constraint(array, pltpu.HBM) for array in arrays])


def solution(mesh):
    placed = (
        P("prompt", "comp"),
        P("prompt", None),
        P("comp", "prompt"),
        P("comp", None, "prompt"),
        P("comp", None, "prompt"),
        P("comp", None, None),
        P("prompt", "comp", None),
        P("comp"),
        P(),
        P(),
        P(),
        P("prompt"),
    )
    return jax.shard_map(
        local, mesh=mesh, in_specs=placed, out_specs=P("comp", None, "prompt"), check_vma=False
    )
```
